32 devices in a mesh: gx: 8 (over z, core), gy: 4 (over y, x).
Axes of the slice: x: 2, y: 2, z: 4, core: 2. Of those that a mesh axis runs over, the one named last changes fastest.
Arguments:
- signal: float32 [32768, 128], P(('gx', 'gy')), may hold values from -6 to 6
- filter_taps: float32 [32768, 128], P(('gx', 'gy')), may hold values from -6 to 6
- grad_out: float32 [32768, 128], P(('gx', 'gy')), may hold values from -0.03125 to 0.03125
Outputs:
- grad_signal: float32 [32768, 128], P(('gx', 'gy'))
- grad_filter: float32 [32768, 128], P(('gx', 'gy'))
The draws below stay inside these ranges and needn't reach their ends.
All inputs are finite; a program needn't handle non-finite values.
Results may differ from the reference program's by a relative error of at most 0.000098.
Values sent between devices are 32-bit elements; how exact they have to be, the bound alone decides.
A program may use at most 128 MiB of HBM per device.

```python
import jax
import jax.numpy as jnp

CH = 128
SEQ = 32768


def level_of(rng, dims, cuts, smallest, largest):
    factor_of, own = 1.0, jax.random.fold_in(rng, 6)
    for axis_at, blocks in cuts:
        heights = jnp.exp(jax.random.uniform(jax.random.fold_in(own, axis_at), (blocks,), jnp.float32, smallest / len(cuts), largest / len(cuts)))
        factor_of = factor_of * jnp.repeat(heights, dims[axis_at] // blocks).reshape([-1 if axis == axis_at else 1 for axis in range(len(dims))])
    return factor_of


def gaussian(stream_key, dims, width, bound, pieces=(), held_as=jnp.bfloat16):
    gain = level_of(stream_key, dims, pieces, -0.22, 0.18) if pieces else 1.0
    result = jax.random.normal(stream_key, dims, jnp.float32) * width * gain
    return jnp.minimum(jnp.maximum(result, -bound), bound).astype(held_as)


def setup_inputs(seed: int = 0) -> dict:
    keys = jax.random.split(jax.random.key(seed), 4)
    return {
        "signal": gaussian(keys[0], (SEQ, CH), 1.0, 6.0, ((0, 32),), jnp.float32),
        "filter_taps": gaussian(keys[1], (SEQ, CH), 1.0, 6.0, ((0, 32),), jnp.float32),
        "grad_out": gaussian(keys[2], (SEQ, CH), SEQ ** -0.5, 0.03125, ((0, 32),), jnp.float32),
    }


def reference(signal, filter_taps, grad_out):
    length = signal.shape[0]
    padded_length = 2 * length
    spec_signal = jnp.fft.fft(signal, n=padded_length, axis=0)
    spec_filter = jnp.fft.fft(filter_taps, n=padded_length, axis=0)
    spec_grad = jnp.fft.fft(grad_out, n=padded_length, axis=0)
    prod_signal = jnp.conj(spec_filter) * spec_grad
    prod_filter = jnp.conj(spec_signal) * spec_grad
    grad_signal = jnp.fft.ifft(prod_signal, axis=0)[:length].real.astype(jnp.float32)
    grad_filter = jnp.fft.ifft(prod_filter, axis=0)[:length].real.astype(jnp.float32)
    return grad_signal, grad_filter
```

```python
import functools
import math

import jax
import jax.numpy as jnp
import numpy as np
from jax import lax
from jax.experimental import pallas as pl
from jax.experimental.pallas import tpu as pltpu
from jax.sharding import PartitionSpec as P

LANES = 128
f32, bf16 = jnp.float32, jnp.bfloat16


def halves(table):
    high = table.astype(np.float32).astype(bf16)
    low = (table - high.astype(np.float64)).astype(np.float32).astype(bf16)
    return np.stack([high, low])


def make_tables(rows):
    first = 2 * rows
    period = first * LANES
    angle = 2.0 * math.pi / first * (np.arange(first)[:, None] * np.arange(rows)[None, :] % first)
    c, s = np.cos(angle), np.sin(angle)
    outer = np.block([[c, -s], [s, c]])
    final = np.block([[c.T, -s.T], [s.T, c.T]]) / period
    lane = np.arange(LANES)
    angle = 2.0 * math.pi / LANES * (lane[:, None] * lane[None, :] % LANES)
    c, s = np.cos(angle), np.sin(angle)
    inner = np.block([[c, s], [-s, c]])
    angle = 2.0 * math.pi / period * (np.arange(first)[:, None] * lane[None, :] % period)
    turn = np.stack([np.cos(angle), np.sin(angle)]).astype(np.float32)
    return halves(outer), halves(final), halves(inner), turn


def split(value):
    high = value.astype(bf16)
    return high, (value - high.astype(f32)).astype(bf16)


def mm(a, b):
    return jnp.dot(a, b, preferred_element_type=f32)


class Plan:
    def __init__(self, devices, channels):
        self.devices, self.channels = devices, channels
        self.group = devices // 4
        self.half = 2 * self.group
        self.each = channels // self.group
        self.whole = self.each // 8
        big = self.each // 2
        small = self.each - self.whole - big
        self.counts = (big, self.whole + small, big, small)
        self.rounds = max(self.counts)
        self.offsets = (self.whole, big, self.whole, self.whole + big)

    def channel(self, quarter, place, r):
        offset = self.offsets[quarter] + r
        if quarter == 1 and self.whole:
            offset = jnp.where(r < self.whole, r, offset)
        return place * self.each + offset


def correlate(role, load, store, rows, tables, scratch):
    outer_ref, final_ref, inner_ref, turn_ref = tables
    zh_ref, zl_ref, gh_ref, gl_ref, yh_ref, yl_ref = scratch
    first = 2 * rows
    z_parts = (0,) if role == "lower" else (0, 1)
    g_parts = {"lower": (0,), "upper": (1,), "full": (0, 1)}[role]
    z_width, g_width = len(z_parts) * LANES, len(g_parts) * LANES
    y_width = z_width
    for n, b in enumerate(z_parts):
        at = slice(n * LANES, (n + 1) * LANES)
        for q in range(2):
            down = slice(q * rows, (q + 1) * rows)
            zh_ref[down, at], zl_ref[down, at] = split(load(b, q))
    for n, b in enumerate(g_parts):
        at = slice(n * LANES, (n + 1) * LANES)
        gh_ref[:, at], gl_ref[:, at] = split(load(b, 2))

    def left(table_ref, at, depth, high_ref, low_ref, width):
        high, low = high_ref[:, :width], low_ref[:, :width]
        return (
            mm(table_ref[0, at, :depth], high)
            + mm(table_ref[0, at, :depth], low)
            + mm(table_ref[1, at, :depth], high)
        )

    def right(value):
        high, low = split(value)
        return mm(high, inner_ref[0]) + mm(low, inner_ref[0]) + mm(high, inner_ref[1])

    block = min(first, 256)

    def step(begin):
        real_rows, imag_rows = pl.ds(begin, block), pl.ds(first + begin, block)
        cosine, sine = turn_ref[0, real_rows, :], turn_ref[1, real_rows, :]
        odd = lax.broadcasted_iota(jnp.int32, (block, 2 * LANES), 0) % 2 == 1

        def rotate(real, imag):
            return jnp.concatenate(
                [real * cosine - imag * sine, real * sine + imag * cosine], axis=1
            )

        def spectra(parts, depth, high_ref, low_ref):
            width = len(parts) * LANES
            real = left(outer_ref, real_rows, depth, high_ref, low_ref, width)
            imag = left(outer_ref, imag_rows, depth, high_ref, low_ref, width)
            found = {}
            for n, b in enumerate(parts):
                at = slice(n * LANES, (n + 1) * LANES)
                found[b] = right(rotate(real[:, at], imag[:, at]))
            return found

        z = spectra(z_parts, 2 * rows, zh_ref, zl_ref)
        g = spectra(g_parts, rows, gh_ref, gl_ref)

        def times(z, g):
            zr, zi, gr, gi = z[:, :LANES], z[:, LANES:], g[:, :LANES], g[:, LANES:]
            return jnp.concatenate([zr * gr + zi * gi, zi * gr - zr * gi], axis=1)

        if role == "lower":
            products = [times(z[0], g[0])]
        else:
            across = times(z[0], g[1])
            inside = times(z[1], g[1])
            if role == "full":
                inside = inside + times(z[0], g[0])
            products = [inside + jnp.where(odd, -across, across), across]
        for n, y in enumerate(products):
            y = right(y)
            y = rotate(y[:, :LANES], y[:, LANES:])
            high, low = split(y)
            at = slice(n * LANES, (n + 1) * LANES)
            yh_ref[real_rows, at], yl_ref[real_rows, at] = high[:, :LANES], low[:, :LANES]
            yh_ref[imag_rows, at], yl_ref[imag_rows, at] = high[:, LANES:], low[:, LANES:]

    if block == first:
        step(0)
    else:

        @pl.loop(0, first // block)
        def _(i):
            step(pl.multiple_of(i * block, block))

    block = min(rows, 128)
    for begin in range(0, 2 * rows, block):
        y = left(final_ref, slice(begin, begin + block), 2 * first, yh_ref, yl_ref, y_width)
        for n in range(len(z_parts)):
            store(n, begin // rows, begin % rows, y[:, n * LANES : (n + 1) * LANES])


def kernel(
    columns,
    plan,
    signal_hbm,
    filter_hbm,
    grad_hbm,
    outer_hbm,
    final_hbm,
    inner_hbm,
    turn_hbm,
    land,
    block_ref,
    send,
    recv,
    back,
    outer_ref,
    final_ref,
    inner_ref,
    turn_ref,
    zh_ref,
    zl_ref,
    gh_ref,
    gl_ref,
    yh_ref,
    yl_ref,
    block_sem,
    table_sem,
    send_sem,
    recv_sem,
    back_sem,
    land_sem,
    own_sem,
):
    devices, group, half = plan.devices, plan.group, plan.half
    height = recv.shape[1]
    tiles = height // 3
    rows = half * tiles
    channels = plan.channels
    me = lax.axis_index("gx") * columns + lax.axis_index("gy")
    quarter, place = me // group, me % group
    is_lower = quarter < 2

    def device(peer):
        return (peer // columns, peer % columns)

    blocks = [
        pltpu.make_async_copy(ref, block_ref.at[q], block_sem.at[q])
        for q, ref in enumerate((filter_hbm, signal_hbm, grad_hbm))
    ]
    for copy in blocks:
        copy.start()
    barrier = pltpu.get_barrier_semaphore()

    @pl.loop(1, devices)
    def _(i):
        pl.semaphore_signal(
            barrier,
            inc=1,
            device_id=device((me + i) % devices),
            device_id_type=pl.DeviceIdType.MESH,
        )

    tables = [
        pltpu.make_async_copy(a, b, table_sem.at[n])
        for n, (a, b) in enumerate(
            (
                (outer_hbm, outer_ref),
                (final_hbm, final_ref),
                (inner_hbm, inner_ref),
                (turn_hbm, turn_ref),
            )
        )
    ]
    for copy in tables:
        copy.start()
    for q in range(3):
        blocks[q].wait()
        for j in range(tiles):
            block = block_ref[q, j * LANES : (j + 1) * LANES, :].T
            send[pl.ds(q * tiles + j, channels, stride=height), :] = block

    def outgoing(target, other, r, size):
        at = pl.multiple_of(plan.channel(target, other, r) * height, tiles)
        return pltpu.make_async_remote_copy(
            src_ref=send.at[pl.ds(at, size), :],
            dst_ref=recv.at[r * devices + me, pl.ds(0, size), :],
            send_sem=send_sem.at[target],
            recv_sem=recv_sem.at[r, jnp.where(is_lower, 0, 1)],
            device_id=device(target * group + other),
            device_id_type=pl.DeviceIdType.MESH,
        )

    def send_round(r):
        def to(target, other, i, size, own):
            limit = plan.counts[target]
            wanted = r < limit
            if own:
                wanted = wanted & ((quarter != target) | (i != 0))

            @pl.when(wanted)
            def _():
                outgoing(target, other, r, size).start()

        @pl.when(is_lower)
        def _():
            @pl.loop(0, group)
            def _(i):
                other = (place + i) % group
                to(2, other, i, 2 * tiles, False)
                to(3, other, i, 2 * tiles, False)
                to(1, other, i, height, True)
                to(0, other, i, height, True)

        @pl.when(jnp.logical_not(is_lower))
        def _():
            @pl.loop(0, group)
            def _(i):
                other = (place + i) % group
                if plan.whole:

                    @pl.when(r < plan.whole)
                    def _():
                        outgoing(1, other, r, height).start()

                to(2, other, i, height, True)
                to(3, other, i, height, True)

    pl.semaphore_wait(barrier, devices - 1)

    @pl.loop(0, plan.rounds)
    def _(r):
        send_round(r)

    for mine in range(4):

        @pl.when(quarter == mine)
        def _():
            @pl.loop(0, plan.counts[mine])
            def _(r):
                at = pl.multiple_of(plan.channel(mine, place, r) * height, tiles)
                recv[r * devices + me] = send[pl.ds(at, height), :]

    for copy in tables:
        copy.wait()

    def returning(mine, r, peer, slot):
        at = pl.multiple_of(plan.channel(mine, place, r) * tiles, tiles)
        return pltpu.make_async_remote_copy(
            src_ref=back.at[r * devices + peer],
            dst_ref=land.at[slot, :, pl.ds(at, tiles), :],
            send_sem=back_sem,
            recv_sem=land_sem.at[slot],
            device_id=device(peer),
            device_id_type=pl.DeviceIdType.MESH,
        )

    def keep(mine, r):
        at = pl.multiple_of(plan.channel(mine, place, r) * tiles, tiles)
        return pltpu.make_async_copy(
            back.at[r * devices + me], land.at[0, :, pl.ds(at, tiles), :], own_sem
        )

    def arrived(r, source_half, count, size):
        ref = recv.at[pl.ds(0, count), pl.ds(0, size), :]
        pltpu.make_async_copy(ref, ref, recv_sem.at[r, source_half]).wait()

    table_refs = (outer_ref, final_ref, inner_ref, turn_ref)
    scratch = (zh_ref, zl_ref, gh_ref, gl_ref, yh_ref, yl_ref)

    def work(role, r):
        def load(b, q):
            at = pl.ds(r * devices + b * half, half)
            return recv[at, q * tiles : (q + 1) * tiles, :].reshape(rows, LANES)

        def store(n, output, begin, value):
            count = value.shape[0] // tiles
            at = pl.ds(r * devices + n * half + begin // tiles, count)
            back[at, output] = value.reshape(count, tiles, LANES)

        correlate(role, load, store, rows, table_refs, scratch)

    def near(mine, r):
        base = me // half * half

        @pl.loop(1, half)
        def _(i):
            returning(mine, r, base + (me + i) % half, 0).start()

        keep(mine, r).start()

    def far(mine, r, slot):
        base = half - me // half * half

        @pl.loop(0, half)
        def _(i):
            returning(mine, r, base + (me + i) % half, slot).start()

    @pl.when(quarter == 0)
    def _():
        @pl.loop(0, plan.counts[0])
        def _(r):
            arrived(r, 0, half - 1, height)
            work("lower", r)
            near(0, r)

    @pl.when(quarter == 1)
    def _():
        if plan.whole:

            @pl.loop(0, plan.whole)
            def _(r):
                arrived(r, 0, half - 1, height)
                arrived(r, 1, half, height)
                work("full", r)
                near(1, r)

        @pl.loop(plan.whole, plan.counts[1])
        def _(r):
            arrived(r, 0, half - 1, height)
            work("lower", r)
            near(1, r)

        if plan.whole:

            @pl.loop(0, plan.whole)
            def _(r):
                far(1, r, 0)

    @pl.when(jnp.logical_not(is_lower))
    def _():
        count = jnp.where(quarter == 2, plan.counts[2], plan.counts[3])

        @pl.loop(0, plan.rounds)
        def _(r):
            @pl.when(r < count)
            def _():
                arrived(r, 0, half, 2 * tiles)
                arrived(r, 1, half - 1, height)
                work("upper", r)
                for mine in (2, 3):

                    @pl.when(quarter == mine)
                    def _():
                        far(mine, r, 1)
                        near(mine, r)

    def finish(ref, sem):
        pltpu.make_async_copy(ref, ref, sem).wait()

    for mine in range(4):

        @pl.when(quarter == mine)
        def _():
            count = plan.counts[mine]
            finish(land.at[0, :, pl.ds(0, count * tiles), :], own_sem)
            finish(land.at[0, :, pl.ds(0, (channels - count) * tiles), :], land_sem.at[0])
            shared = channels - group * plan.whole
            if mine < 2:
                finish(land.at[1, :, pl.ds(0, shared * tiles), :], land_sem.at[1])
            returned = count * (half - 1)
            if mine == 1:
                returned += plan.whole * half
            elif mine > 1:
                returned += count * half
            finish(back.at[pl.ds(0, returned)], back_sem)
            for target in range(4):
                size = 2 * tiles if mine < 2 and target >= 2 else height
                sent = plan.counts[target] * (group - (mine == target))
                if mine >= 2 and target < 2:
                    sent = plan.whole * group * target
                if sent:
                    finish(recv.at[pl.ds(0, sent), pl.ds(0, size), :], send_sem.at[target])


def spread_kernel(columns, plan, land, out0_ref, out1_ref, land_ref, result_ref, in_sem, out_sem):
    _, rows_local, channels = result_ref.shape
    tiles = rows_local // LANES
    me = lax.axis_index("gx") * columns + lax.axis_index("gy")
    is_lower = me < plan.half

    def read(slot, q):
        return pltpu.make_async_copy(land.at[slot, q], land_ref.at[slot, q], in_sem.at[slot, q])

    for q in range(2):
        read(0, q).start()

        @pl.when(is_lower)
        def _():
            read(1, q).start()

    half = rows_local // 2
    shared = lax.broadcasted_iota(jnp.int32, (channels, LANES), 0) % plan.each >= plan.whole

    def run(slots):
        writes = []
        for q, ref in enumerate((out0_ref, out1_ref)):
            for slot in range(slots):
                read(slot, q).wait()
            for j in range(tiles):
                block = land_ref[0, q, pl.ds(j, channels, stride=tiles), :]
                if slots == 2:
                    more = land_ref[1, q, pl.ds(j, channels, stride=tiles), :]
                    block = block + jnp.where(shared, more, 0.0)
                result_ref[q, j * LANES : (j + 1) * LANES, :] = block.T
                if (j + 1) % (tiles // 2) == 0:
                    at = slice((j + 1) * LANES - half, (j + 1) * LANES)
                    writes.append(
                        pltpu.make_async_copy(
                            result_ref.at[q, at, :], ref.at[at, :], out_sem.at[len(writes)]
                        )
                    )
                    writes[-1].start()
        for copy in writes:
            copy.wait()

    @pl.when(is_lower)
    def _():
        run(2)

    @pl.when(jnp.logical_not(is_lower))
    def _():
        run(1)


def shards(signal, filter_taps, grad_out):
    rows_local, channels = signal.shape
    columns = lax.axis_size("gy")
    devices = lax.axis_size("gx") * columns
    tiles = rows_local // LANES
    plan = Plan(devices, channels)
    rows = plan.half * tiles
    outer, final, inner, turn = make_tables(rows)
    anywhere = pl.BlockSpec(memory_space=pl.ANY)
    result = jax.ShapeDtypeStruct((rows_local, channels), f32)
    land = pl.pallas_call(
        functools.partial(kernel, columns, plan),
        out_shape=jax.ShapeDtypeStruct((2, 2, channels * tiles, LANES), f32),
        in_specs=[anywhere] * 7,
        out_specs=anywhere,
        scratch_shapes=[
            pltpu.VMEM((3, rows_local, channels), f32),
            pltpu.VMEM((channels * 3 * tiles, LANES), f32),
            pltpu.VMEM((plan.rounds * devices, 3 * tiles, LANES), f32),
            pltpu.VMEM((plan.rounds * devices, 2, tiles, LANES), f32),
            pltpu.VMEM(outer.shape, bf16),
            pltpu.VMEM(final.shape, bf16),
            pltpu.VMEM(inner.shape, bf16),
            pltpu.VMEM(turn.shape, f32),
            pltpu.VMEM((2 * rows, 2 * LANES), bf16),
            pltpu.VMEM((2 * rows, 2 * LANES), bf16),
            pltpu.VMEM((rows, 2 * LANES), bf16),
            pltpu.VMEM((rows, 2 * LANES), bf16),
            pltpu.VMEM((4 * rows, 2 * LANES), bf16),
            pltpu.VMEM((4 * rows, 2 * LANES), bf16),
            pltpu.SemaphoreType.DMA((3,)),
            pltpu.SemaphoreType.DMA((4,)),
            pltpu.SemaphoreType.DMA((4,)),
            pltpu.SemaphoreType.DMA((plan.rounds, 2)),
            pltpu.SemaphoreType.DMA,
            pltpu.SemaphoreType.DMA((2,)),
            pltpu.SemaphoreType.DMA,
        ],
        compiler_params=pltpu.CompilerParams(
            collective_id=0, has_side_effects=True, vmem_limit_bytes=60 << 20
        ),
    )(signal, filter_taps, grad_out, outer, final, inner, turn)
    return pl.pallas_call(
        functools.partial(spread_kernel, columns, plan),
        out_shape=(result, result),
        in_specs=[anywhere],
        out_specs=(anywhere, anywhere),
        scratch_shapes=[
            pltpu.VMEM((2, 2, channels * tiles, LANES), f32),
            pltpu.VMEM((2, rows_local, channels), f32),
            pltpu.SemaphoreType.DMA((2, 2)),
            pltpu.SemaphoreType.DMA((4,)),
        ],
        compiler_params=pltpu.CompilerParams(vmem_limit_bytes=60 << 20),
    )(land)


def solution(mesh):
    spec = P(("gx", "gy"), None)
    return jax.shard_map(
        shards, mesh=mesh, in_specs=(spec,) * 3, out_specs=(spec,) * 2, check_vma=False
    )
```

```python
import functools
import math

import jax
import jax.numpy as jnp
import numpy as np
from jax import lax
from jax.experimental import pallas as pl
from jax.experimental.pallas import tpu as pltpu
from jax.sharding import PartitionSpec as P

LANES = 128
f32, bf16 = jnp.float32, jnp.bfloat16
AHEAD = 4
FAR_AFTER = 4


def halves(table):
    high = table.astype(np.float32).astype(bf16)
    low = (table - high.astype(np.float64)).astype(np.float32).astype(bf16)
    return np.stack([high, low])


def make_tables(rows):
    first = 2 * rows
    period = first * LANES
    angle = 2.0 * math.pi / first * (np.arange(first)[:, None] * np.arange(rows)[None, :] % first)
    c, s = np.cos(angle), np.sin(angle)
    outer = np.block([[c, -s], [s, c]])
    final = np.block([[c.T, -s.T], [s.T, c.T]]) / period
    lane = np.arange(LANES)
    angle = 2.0 * math.pi / LANES * (lane[:, None] * lane[None, :] % LANES)
    c, s = np.cos(angle), np.sin(angle)
    inner = np.block([[c, s], [-s, c]])
    angle = 2.0 * math.pi / period * (np.arange(first)[:, None] * lane[None, :] % period)
    turn = np.stack([np.cos(angle), np.sin(angle)]).astype(np.float32)
    return halves(outer), halves(final), halves(inner), turn


def split(value):
    high = value.astype(bf16)
    return high, (value - high.astype(f32)).astype(bf16)


def mm(a, b):
    return jnp.dot(a, b, preferred_element_type=f32)


class Plan:
    def __init__(self, devices, channels):
        self.devices, self.channels = devices, channels
        self.group = devices // 4
        self.half = 2 * self.group
        self.each = channels // self.group
        self.whole = self.each // 8
        big = self.each // 2
        small = self.each - self.whole - big
        self.counts = (big, self.whole + small, big, small)
        self.rounds = max(self.counts)
        self.offsets = (self.whole, big, self.whole, self.whole + big)

    def channel(self, quarter, place, r):
        offset = self.offsets[quarter] + r
        if quarter == 1 and self.whole:
            offset = jnp.where(r < self.whole, r, offset)
        return place * self.each + offset


def correlate(role, load, store, rows, tables, scratch):
    outer_ref, final_ref, inner_ref, turn_ref = tables
    zh_ref, zl_ref, gh_ref, gl_ref, yh_ref, yl_ref = scratch
    first = 2 * rows
    z_parts = (0,) if role == "lower" else (0, 1)
    g_parts = {"lower": (0,), "upper": (1,), "full": (0, 1)}[role]
    z_width, g_width = len(z_parts) * LANES, len(g_parts) * LANES
    y_width = z_width
    for n, b in enumerate(z_parts):
        at = slice(n * LANES, (n + 1) * LANES)
        for q in range(2):
            down = slice(q * rows, (q + 1) * rows)
            zh_ref[down, at], zl_ref[down, at] = split(load(b, q))
    for n, b in enumerate(g_parts):
        at = slice(n * LANES, (n + 1) * LANES)
        gh_ref[:, at], gl_ref[:, at] = split(load(b, 2))

    def left(table_ref, at, depth, high_ref, low_ref, width):
        high, low = high_ref[:, :width], low_ref[:, :width]
        return (
            mm(table_ref[0, at, :depth], high)
            + mm(table_ref[0, at, :depth], low)
            + mm(table_ref[1, at, :depth], high)
        )

    def right(value):
        high, low = split(value)
        return mm(high, inner_ref[0]) + mm(low, inner_ref[0]) + mm(high, inner_ref[1])

    block = min(first, 256)

    def step(begin):
        real_rows, imag_rows = pl.ds(begin, block), pl.ds(first + begin, block)
        cosine, sine = turn_ref[0, real_rows, :], turn_ref[1, real_rows, :]
        odd = lax.broadcasted_iota(jnp.int32, (block, 2 * LANES), 0) % 2 == 1

        def rotate(real, imag):
            return jnp.concatenate(
                [real * cosine - imag * sine, real * sine + imag * cosine], axis=1
            )

        def spectra(parts, depth, high_ref, low_ref):
            width = len(parts) * LANES
            real = left(outer_ref, real_rows, depth, high_ref, low_ref, width)
            imag = left(outer_ref, imag_rows, depth, high_ref, low_ref, width)
            found = {}
            for n, b in enumerate(parts):
                at = slice(n * LANES, (n + 1) * LANES)
                found[b] = right(rotate(real[:, at], imag[:, at]))
            return found

        z = spectra(z_parts, 2 * rows, zh_ref, zl_ref)
        g = spectra(g_parts, rows, gh_ref, gl_ref)

        def times(z, g):
            zr, zi, gr, gi = z[:, :LANES], z[:, LANES:], g[:, :LANES], g[:, LANES:]
            return jnp.concatenate([zr * gr + zi * gi, zi * gr - zr * gi], axis=1)

        if role == "lower":
            products = [times(z[0], g[0])]
        else:
            across = times(z[0], g[1])
            inside = times(z[1], g[1])
            if role == "full":
                inside = inside + times(z[0], g[0])
            products = [inside + jnp.where(odd, -across, across), across]
        for n, y in enumerate(products):
            y = right(y)
            y = rotate(y[:, :LANES], y[:, LANES:])
            high, low = split(y)
            at = slice(n * LANES, (n + 1) * LANES)
            yh_ref[real_rows, at], yl_ref[real_rows, at] = high[:, :LANES], low[:, :LANES]
            yh_ref[imag_rows, at], yl_ref[imag_rows, at] = high[:, LANES:], low[:, LANES:]

    if block == first:
        step(0)
    else:

        @pl.loop(0, first // block)
        def _(i):
            step(pl.multiple_of(i * block, block))

    block = min(rows, 128)
    for begin in range(0, 2 * rows, block):
        y = left(final_ref, slice(begin, begin + block), 2 * first, yh_ref, yl_ref, y_width)
        for n in range(len(z_parts)):
            store(n, begin // rows, begin % rows, y[:, n * LANES : (n + 1) * LANES])


def kernel(
    columns,
    plan,
    signal_hbm,
    filter_hbm,
    grad_hbm,
    outer_hbm,
    final_hbm,
    inner_hbm,
    turn_hbm,
    land,
    block_ref,
    send,
    recv,
    back,
    outer_ref,
    final_ref,
    inner_ref,
    turn_ref,
    zh_ref,
    zl_ref,
    gh_ref,
    gl_ref,
    yh_ref,
    yl_ref,
    block_sem,
    table_sem,
    send_sem,
    recv_sem,
    back_sem,
    land_sem,
    own_sem,
):
    devices, group, half = plan.devices, plan.group, plan.half
    height = recv.shape[1]
    tiles = height // 3
    rows = half * tiles
    channels = plan.channels
    gx, gy = lax.axis_index("gx"), lax.axis_index("gy")
    me = gx * columns + gy
    deep = group // columns
    quarter, level = gx // deep, gx % deep
    place = level * columns + gy
    is_lower = quarter < 2
    across = [(gy + b) % columns for b in range(columns)]

    def device(peer):
        return (peer // columns, peer % columns)

    def places(body):
        @pl.loop(0, deep)
        def _(a):
            other_level = lax.rem(level + a, deep)
            for b in range(columns):
                body(a == 0 if b == 0 else None, other_level, across[b], other_level * columns + across[b])

    blocks = [
        pltpu.make_async_copy(ref, block_ref.at[q], block_sem.at[q])
        for q, ref in enumerate((filter_hbm, signal_hbm, grad_hbm))
    ]
    for copy in blocks:
        copy.start()
    barrier = pltpu.get_barrier_semaphore()

    @pl.loop(1, devices)
    def _(i):
        pl.semaphore_signal(
            barrier,
            inc=1,
            device_id=device((me + i) % devices),
            device_id_type=pl.DeviceIdType.MESH,
        )

    tables = [
        pltpu.make_async_copy(a, b, table_sem.at[n])
        for n, (a, b) in enumerate(
            (
                (outer_hbm, outer_ref),
                (final_hbm, final_ref),
                (inner_hbm, inner_ref),
                (turn_hbm, turn_ref),
            )
        )
    ]
    for copy in tables:
        copy.start()
    for q in range(3):
        blocks[q].wait()
        for j in range(tiles):
            block = block_ref[q, j * LANES : (j + 1) * LANES, :].T
            send[pl.ds(q * tiles + j, channels, stride=height), :] = block

    def send_to(target, r, size):
        row = plan.channel(target, 0, r) * height
        arrival = recv.at[r * devices + me, pl.ds(0, size), :]
        sem = recv_sem.at[r, jnp.where(is_lower, 0, 1)]

        def body(same, other_level, other_gy, other):
            def start():
                at = pl.multiple_of(other * (plan.each * height) + row, tiles)
                pltpu.make_async_remote_copy(
                    src_ref=send.at[pl.ds(at, size), :],
                    dst_ref=arrival,
                    send_sem=send_sem.at[target],
                    recv_sem=sem,
                    device_id=(target * deep + other_level, other_gy),
                    device_id_type=pl.DeviceIdType.MESH,
                ).start()

            if same is None:
                start()
            else:
                pl.when(jnp.logical_not(same & (quarter == target)))(start)

        return body

    def send_round(r):
        def guarded(bounds, targets, sizes):
            for target, bound, size in zip(targets, bounds, sizes):
                if bound:

                    @pl.when(r < bound)
                    def _():
                        places(send_to(target, r, size))

        @pl.when(is_lower)
        def _():
            counts = plan.counts
            guarded(
                (counts[2], counts[3], counts[1], counts[0]),
                (2, 3, 1, 0),
                (2 * tiles, 2 * tiles, height, height),
            )

        @pl.when(jnp.logical_not(is_lower))
        def _():
            guarded((plan.whole, *plan.counts[2:]), (1, 2, 3), (height,) * 3)

    pl.semaphore_wait(barrier, devices - 1)

    @pl.loop(0, min(AHEAD, plan.rounds))
    def _(r):
        send_round(r)

    for mine in range(4):

        @pl.when(quarter == mine)
        def _():
            @pl.loop(0, plan.counts[mine])
            def _(r):
                at = pl.multiple_of(plan.channel(mine, place, r) * height, tiles)
                recv[r * devices + me] = send[pl.ds(at, height), :]

    for copy in tables:
        copy.wait()

    def return_to(mine, r, target, slot):
        at = pl.multiple_of(plan.channel(mine, place, r) * tiles, tiles)
        landing = land.at[slot, :, pl.ds(at, tiles), :]
        base = r * devices + target * group

        def body(same, other_level, other_gy, other):
            def start():
                pltpu.make_async_remote_copy(
                    src_ref=back.at[base + other],
                    dst_ref=landing,
                    send_sem=back_sem,
                    recv_sem=land_sem.at[slot],
                    device_id=(target * deep + other_level, other_gy),
                    device_id_type=pl.DeviceIdType.MESH,
                ).start()

            if same is None or mine != target:
                start()
            else:
                pl.when(jnp.logical_not(same))(start)

        places(body)

    def keep(mine, r):
        at = pl.multiple_of(plan.channel(mine, place, r) * tiles, tiles)
        return pltpu.make_async_copy(
            back.at[r * devices + me], land.at[0, :, pl.ds(at, tiles), :], own_sem
        )

    def arrived(r, source_half, count, size):
        ref = recv.at[pl.ds(0, count), pl.ds(0, size), :]
        pltpu.make_async_copy(ref, ref, recv_sem.at[r, source_half]).wait()

    table_refs = (outer_ref, final_ref, inner_ref, turn_ref)
    scratch = (zh_ref, zl_ref, gh_ref, gl_ref, yh_ref, yl_ref)

    def work(role, r):
        def load(b, q):
            at = pl.ds(r * devices + b * half, half)
            return recv[at, q * tiles : (q + 1) * tiles, :].reshape(rows, LANES)

        def store(n, output, begin, value):
            count = value.shape[0] // tiles
            at = pl.ds(r * devices + n * half + begin // tiles, count)
            back[at, output] = value.reshape(count, tiles, LANES)

        correlate(role, load, store, rows, table_refs, scratch)

    def near(mine, r):
        for target in ((0, 1) if mine < 2 else (2, 3)):
            return_to(mine, r, target, 0)
        keep(mine, r).start()

    def far(mine, r, slot):
        for target in ((2, 3) if mine < 2 else (0, 1)):
            return_to(mine, r, target, slot)

    def next_round(r):
        @pl.when(r + AHEAD < plan.rounds)
        def _():
            send_round(r + AHEAD)

    def only(mine, r, body):
        count = plan.counts[mine]
        pl.when((quarter == mine) & (r < count) if count < plan.rounds else quarter == mine)(body)

    @pl.loop(0, plan.rounds)
    def _(r):
        @pl.when(is_lower)
        def _():
            def lower(mine):
                def body():
                    arrived(r, 0, half - 1, height)

                only(mine, r, body)

            lower(0)
            lower(1)
            full = (quarter == 1) & (r < plan.whole)
            if plan.whole:

                @pl.when(full)
                def _():
                    arrived(r, 1, half, height)
                    work("full", r)

            @pl.when(jnp.logical_not(full) & (r < jnp.where(quarter == 0, plan.counts[0], plan.counts[1])))
            def _():
                work("lower", r)

            only(0, r, lambda: near(0, r))
            only(1, r, lambda: near(1, r))
            if plan.whole:
                late = min(FAR_AFTER, plan.rounds - plan.whole)

                @pl.when((quarter == 1) & (r >= late) & (r < late + plan.whole))
                def _():
                    far(1, r - late, 0)

        @pl.when(jnp.logical_not(is_lower))
        def _():
            @pl.when(r < jnp.where(quarter == 2, plan.counts[2], plan.counts[3]))
            def _():
                arrived(r, 0, half, 2 * tiles)
                arrived(r, 1, half - 1, height)
                work("upper", r)

            def upper(mine):
                def body():
                    far(mine, r, 1)
                    near(mine, r)

                only(mine, r, body)

            upper(2)
            upper(3)

        next_round(r)

    def finish(ref, sem):
        pltpu.make_async_copy(ref, ref, sem).wait()

    for mine in range(4):

        @pl.when(quarter == mine)
        def _():
            count = plan.counts[mine]
            finish(land.at[0, :, pl.ds(0, count * tiles), :], own_sem)
            finish(land.at[0, :, pl.ds(0, (channels - count) * tiles), :], land_sem.at[0])
            shared = channels - group * plan.whole
            if mine < 2:
                finish(land.at[1, :, pl.ds(0, shared * tiles), :], land_sem.at[1])
            returned = count * (half - 1)
            if mine == 1:
                returned += plan.whole * half
            elif mine > 1:
                returned += count * half
            finish(back.at[pl.ds(0, returned)], back_sem)
            for target in range(4):
                size = 2 * tiles if mine < 2 and target >= 2 else height
                sent = plan.counts[target] * (group - (mine == target))
                if mine >= 2 and target < 2:
                    sent = plan.whole * group * target
                if sent:
                    finish(recv.at[pl.ds(0, sent), pl.ds(0, size), :], send_sem.at[target])


def spread_kernel(columns, plan, land, out0_ref, out1_ref, land_ref, result_ref, in_sem, out_sem):
    _, rows_local, channels = result_ref.shape
    tiles = rows_local // LANES
    me = lax.axis_index("gx") * columns + lax.axis_index("gy")
    is_lower = me < plan.half

    def read(slot, q):
        return pltpu.make_async_copy(land.at[slot, q], land_ref.at[slot, q], in_sem.at[slot, q])

    for q in range(2):
        read(0, q).start()

        @pl.when(is_lower)
        def _():
            read(1, q).start()

    half = rows_local // 2
    shared = lax.broadcasted_iota(jnp.int32, (channels, LANES), 0) % plan.each >= plan.whole

    def run(slots):
        writes = []
        for q, ref in enumerate((out0_ref, out1_ref)):
            for slot in range(slots):
                read(slot, q).wait()
            for j in range(tiles):
                block = land_ref[0, q, pl.ds(j, channels, stride=tiles), :]
                if slots == 2:
                    more = land_ref[1, q, pl.ds(j, channels, stride=tiles), :]
                    block = block + jnp.where(shared, more, 0.0)
                result_ref[q, j * LANES : (j + 1) * LANES, :] = block.T
                if (j + 1) % (tiles // 2) == 0:
                    at = slice((j + 1) * LANES - half, (j + 1) * LANES)
                    writes.append(
                        pltpu.make_async_copy(
                            result_ref.at[q, at, :], ref.at[at, :], out_sem.at[len(writes)]
                        )
                    )
                    writes[-1].start()
        for copy in writes:
            copy.wait()

    @pl.when(is_lower)
    def _():
        run(2)

    @pl.when(jnp.logical_not(is_lower))
    def _():
        run(1)


def shards(signal, filter_taps, grad_out):
    rows_local, channels = signal.shape
    columns = lax.axis_size("gy")
    devices = lax.axis_size("gx") * columns
    tiles = rows_local // LANES
    plan = Plan(devices, channels)
    rows = plan.half * tiles
    outer, final, inner, turn = make_tables(rows)
    anywhere = pl.BlockSpec(memory_space=pl.ANY)
    result = jax.ShapeDtypeStruct((rows_local, channels), f32)
    land = pl.pallas_call(
        functools.partial(kernel, columns, plan),
        out_shape=jax.ShapeDtypeStruct((2, 2, channels * tiles, LANES), f32),
        in_specs=[anywhere] * 7,
        out_specs=anywhere,
        scratch_shapes=[
            pltpu.VMEM((3, rows_local, channels), f32),
            pltpu.VMEM((channels * 3 * tiles, LANES), f32),
            pltpu.VMEM((plan.rounds * devices, 3 * tiles, LANES), f32),
            pltpu.VMEM((plan.rounds * devices, 2, tiles, LANES), f32),
            pltpu.VMEM(outer.shape, bf16),
            pltpu.VMEM(final.shape, bf16),
            pltpu.VMEM(inner.shape, bf16),
            pltpu.VMEM(turn.shape, f32),
            pltpu.VMEM((2 * rows, 2 * LANES), bf16),
            pltpu.VMEM((2 * rows, 2 * LANES), bf16),
            pltpu.VMEM((rows, 2 * LANES), bf16),
            pltpu.VMEM((rows, 2 * LANES), bf16),
            pltpu.VMEM((4 * rows, 2 * LANES), bf16),
            pltpu.VMEM((4 * rows, 2 * LANES), bf16),
            pltpu.SemaphoreType.DMA((3,)),
            pltpu.SemaphoreType.DMA((4,)),
            pltpu.SemaphoreType.DMA((4,)),
            pltpu.SemaphoreType.DMA((plan.rounds, 2)),
            pltpu.SemaphoreType.DMA,
            pltpu.SemaphoreType.DMA((2,)),
            pltpu.SemaphoreType.DMA,
        ],
        compiler_params=pltpu.CompilerParams(
            collective_id=0, has_side_effects=True, vmem_limit_bytes=60 << 20
        ),
    )(signal, filter_taps, grad_out, outer, final, inner, turn)
    return pl.pallas_call(
        functools.partial(spread_kernel, columns, plan),
        out_shape=(result, result),
        in_specs=[anywhere],
        out_specs=(anywhere, anywhere),
        scratch_shapes=[
            pltpu.VMEM((2, 2, channels * tiles, LANES), f32),
            pltpu.VMEM((2, rows_local, channels), f32),
            pltpu.SemaphoreType.DMA((2, 2)),
            pltpu.SemaphoreType.DMA((4,)),
        ],
        compiler_params=pltpu.CompilerParams(vmem_limit_bytes=60 << 20),
    )(land)


def solution(mesh):
    spec = P(("gx", "gy"), None)
    return jax.shard_map(
        shards, mesh=mesh, in_specs=(spec,) * 3, out_specs=(spec,) * 2, check_vma=False
    )
```

```python
import functools
import math

import jax
import jax.numpy as jnp
import numpy as np
from jax import lax
from jax.experimental import pallas as pl
from jax.experimental.pallas import tpu as pltpu
from jax.sharding import PartitionSpec as P

LANES = 128
f32, bf16 = jnp.float32, jnp.bfloat16
AHEAD = 4
FAR_AFTER = 4


def halves(table):
    high = table.astype(np.float32).astype(bf16)
    low = (table - high.astype(np.float64)).astype(np.float32).astype(bf16)
    return np.stack([high, low])


def make_tables(rows):
    first = 2 * rows
    period = first * LANES
    angle = 2.0 * math.pi / first * (np.arange(first)[:, None] * np.arange(rows)[None, :] % first)
    c, s = np.cos(angle), np.sin(angle)
    outer = np.block([[c, -s], [s, c]])
    final = np.block([[c.T, -s.T], [s.T, c.T]]) / period
    lane = np.arange(LANES)
    angle = 2.0 * math.pi / LANES * (lane[:, None] * lane[None, :] % LANES)
    c, s = np.cos(angle), np.sin(angle)
    inner = np.block([[c, s], [-s, c]])
    angle = 2.0 * math.pi / period * (np.arange(first)[:, None] * lane[None, :] % period)
    turn = np.stack([np.cos(angle), np.sin(angle)]).astype(np.float32)
    return halves(outer), halves(final), halves(inner), turn


def split(value):
    high = value.astype(bf16)
    return high, (value - high.astype(f32)).astype(bf16)


def mm(a, b):
    return jnp.dot(a, b, preferred_element_type=f32)


class Plan:
    def __init__(self, devices, channels):
        self.devices, self.channels = devices, channels
        self.group = devices // 4
        self.half = 2 * self.group
        self.each = channels // self.group
        self.whole = self.each // 4
        big = self.each // 2
        small = self.each - self.whole - big
        self.counts = (big, self.whole + small, big, small)
        self.rounds = max(self.counts)
        self.offsets = (self.whole, big, self.whole, self.whole + big)

    def channel(self, quarter, place, r):
        offset = self.offsets[quarter] + r
        if quarter == 1 and self.whole:
            offset = jnp.where(r < self.whole, r, offset)
        return place * self.each + offset


def correlate(role, load, store, rows, tables, scratch):
    outer_ref, final_ref, inner_ref, turn_ref = tables
    zh_ref, zl_ref, gh_ref, gl_ref, yh_ref, yl_ref = scratch
    first = 2 * rows
    z_parts = (0,) if role == "lower" else (0, 1)
    g_parts = {"lower": (0,), "upper": (1,), "full": (0, 1)}[role]
    z_width, g_width = len(z_parts) * LANES, len(g_parts) * LANES
    y_width = z_width
    for n, b in enumerate(z_parts):
        at = slice(n * LANES, (n + 1) * LANES)
        for q in range(2):
            down = slice(q * rows, (q + 1) * rows)
            zh_ref[down, at], zl_ref[down, at] = split(load(b, q))
    for n, b in enumerate(g_parts):
        at = slice(n * LANES, (n + 1) * LANES)
        gh_ref[:, at], gl_ref[:, at] = split(load(b, 2))

    def left(table_ref, at, depth, high_ref, low_ref, width):
        high, low = high_ref[:, :width], low_ref[:, :width]
        return (
            mm(table_ref[0, at, :depth], high)
            + mm(table_ref[0, at, :depth], low)
            + mm(table_ref[1, at, :depth], high)
        )

    def right(value):
        high, low = split(value)
        return mm(high, inner_ref[0]) + mm(low, inner_ref[0]) + mm(high, inner_ref[1])

    block = min(first, 256)

    def step(begin):
        real_rows, imag_rows = pl.ds(begin, block), pl.ds(first + begin, block)
        cosine, sine = turn_ref[0, real_rows, :], turn_ref[1, real_rows, :]
        odd = lax.broadcasted_iota(jnp.int32, (block, 2 * LANES), 0) % 2 == 1

        def rotate(real, imag):
            return jnp.concatenate(
                [real * cosine - imag * sine, real * sine + imag * cosine], axis=1
            )

        def spectra(parts, depth, high_ref, low_ref):
            width = len(parts) * LANES
            real = left(outer_ref, real_rows, depth, high_ref, low_ref, width)
            imag = left(outer_ref, imag_rows, depth, high_ref, low_ref, width)
            found = {}
            for n, b in enumerate(parts):
                at = slice(n * LANES, (n + 1) * LANES)
                found[b] = right(rotate(real[:, at], imag[:, at]))
            return found

        z = spectra(z_parts, 2 * rows, zh_ref, zl_ref)
        g = spectra(g_parts, rows, gh_ref, gl_ref)

        def times(z, g):
            zr, zi, gr, gi = z[:, :LANES], z[:, LANES:], g[:, :LANES], g[:, LANES:]
            return jnp.concatenate([zr * gr + zi * gi, zi * gr - zr * gi], axis=1)

        if role == "lower":
            products = [times(z[0], g[0])]
        else:
            across = times(z[0], g[1])
            inside = times(z[1], g[1])
            if role == "full":
                inside = inside + times(z[0], g[0])
            products = [inside + jnp.where(odd, -across, across), across]
        for n, y in enumerate(products):
            y = right(y)
            y = rotate(y[:, :LANES], y[:, LANES:])
            high, low = split(y)
            at = slice(n * LANES, (n + 1) * LANES)
            yh_ref[real_rows, at], yl_ref[real_rows, at] = high[:, :LANES], low[:, :LANES]
            yh_ref[imag_rows, at], yl_ref[imag_rows, at] = high[:, LANES:], low[:, LANES:]

    if block == first:
        step(0)
    else:

        @pl.loop(0, first // block)
        def _(i):
            step(pl.multiple_of(i * block, block))

    block = min(rows, 128)
    for begin in range(0, 2 * rows, block):
        y = left(final_ref, slice(begin, begin + block), 2 * first, yh_ref, yl_ref, y_width)
        for n in range(len(z_parts)):
            store(n, begin // rows, begin % rows, y[:, n * LANES : (n + 1) * LANES])


def kernel(
    columns,
    plan,
    signal_hbm,
    filter_hbm,
    grad_hbm,
    outer_hbm,
    final_hbm,
    inner_hbm,
    turn_hbm,
    land,
    block_ref,
    send,
    recv,
    back,
    outer_ref,
    final_ref,
    inner_ref,
    turn_ref,
    zh_ref,
    zl_ref,
    gh_ref,
    gl_ref,
    yh_ref,
    yl_ref,
    block_sem,
    table_sem,
    send_sem,
    recv_sem,
    back_sem,
    land_sem,
    own_sem,
):
    devices, group, half = plan.devices, plan.group, plan.half
    height = recv.shape[1]
    tiles = height // 3
    rows = half * tiles
    channels = plan.channels
    gx, gy = lax.axis_index("gx"), lax.axis_index("gy")
    me = gx * columns + gy
    deep = group // columns
    quarter, level = gx // deep, gx % deep
    place = level * columns + gy
    is_lower = quarter < 2
    across = [(gy + b) % columns for b in range(columns)]

    def device(peer):
        return (peer // columns, peer % columns)

    def places(body):
        @pl.loop(0, deep)
        def _(a):
            other_level = lax.rem(level + a, deep)
            for b in range(columns):
                body(a == 0 if b == 0 else None, other_level, across[b], other_level * columns + across[b])

    blocks = [
        pltpu.make_async_copy(ref, block_ref.at[q], block_sem.at[q])
        for q, ref in enumerate((filter_hbm, signal_hbm, grad_hbm))
    ]
    for copy in blocks:
        copy.start()
    barrier = pltpu.get_barrier_semaphore()

    @pl.loop(1, devices)
    def _(i):
        pl.semaphore_signal(
            barrier,
            inc=1,
            device_id=device((me + i) % devices),
            device_id_type=pl.DeviceIdType.MESH,
        )

    tables = [
        pltpu.make_async_copy(a, b, table_sem.at[n])
        for n, (a, b) in enumerate(
            (
                (outer_hbm, outer_ref),
                (final_hbm, final_ref),
                (inner_hbm, inner_ref),
                (turn_hbm, turn_ref),
            )
        )
    ]
    for copy in tables:
        copy.start()
    for q in range(3):
        blocks[q].wait()
        for j in range(tiles):
            block = block_ref[q, j * LANES : (j + 1) * LANES, :].T
            send[pl.ds(q * tiles + j, channels, stride=height), :] = block

    def send_to(target, r, size):
        row = plan.channel(target, 0, r) * height
        arrival = recv.at[r * devices + me, pl.ds(0, size), :]
        sem = recv_sem.at[r, jnp.where(is_lower, 0, 1)]

        def body(same, other_level, other_gy, other):
            def start():
                at = pl.multiple_of(other * (plan.each * height) + row, tiles)
                pltpu.make_async_remote_copy(
                    src_ref=send.at[pl.ds(at, size), :],
                    dst_ref=arrival,
                    send_sem=send_sem.at[target],
                    recv_sem=sem,
                    device_id=(target * deep + other_level, other_gy),
                    device_id_type=pl.DeviceIdType.MESH,
                ).start()

            if same is None:
                start()
            else:
                pl.when(jnp.logical_not(same & (quarter == target)))(start)

        return body

    def send_round(r):
        def guarded(bounds, targets, sizes):
            for target, bound, size in zip(targets, bounds, sizes):
                if bound:

                    @pl.when(r < bound)
                    def _():
                        places(send_to(target, r, size))

        @pl.when(is_lower)
        def _():
            counts = plan.counts
            guarded(
                (counts[2], counts[3], counts[1], counts[0]),
                (2, 3, 1, 0),
                (2 * tiles, 2 * tiles, height, height),
            )

        @pl.when(jnp.logical_not(is_lower))
        def _():
            guarded((plan.whole, *plan.counts[2:]), (1, 2, 3), (height,) * 3)

    pl.semaphore_wait(barrier, devices - 1)

    @pl.loop(0, min(AHEAD, plan.rounds))
    def _(r):
        send_round(r)

    for mine in range(4):

        @pl.when(quarter == mine)
        def _():
            @pl.loop(0, plan.counts[mine])
            def _(r):
                at = pl.multiple_of(plan.channel(mine, place, r) * height, tiles)
                recv[r * devices + me] = send[pl.ds(at, height), :]

    for copy in tables:
        copy.wait()

    def return_to(mine, r, target, slot):
        at = pl.multiple_of(plan.channel(mine, place, r) * tiles, tiles)
        landing = land.at[slot, :, pl.ds(at, tiles), :]
        base = r * devices + target * group

        def body(same, other_level, other_gy, other):
            def start():
                pltpu.make_async_remote_copy(
                    src_ref=back.at[base + other],
                    dst_ref=landing,
                    send_sem=back_sem,
                    recv_sem=land_sem.at[slot],
                    device_id=(target * deep + other_level, other_gy),
                    device_id_type=pl.DeviceIdType.MESH,
                ).start()

            if same is None or mine != target:
                start()
            else:
                pl.when(jnp.logical_not(same))(start)

        places(body)

    def keep(mine, r):
        at = pl.multiple_of(plan.channel(mine, place, r) * tiles, tiles)
        return pltpu.make_async_copy(
            back.at[r * devices + me], land.at[0, :, pl.ds(at, tiles), :], own_sem
        )

    def arrived(r, source_half, count, size):
        ref = recv.at[pl.ds(0, count), pl.ds(0, size), :]
        pltpu.make_async_copy(ref, ref, recv_sem.at[r, source_half]).wait()

    table_refs = (outer_ref, final_ref, inner_ref, turn_ref)
    scratch = (zh_ref, zl_ref, gh_ref, gl_ref, yh_ref, yl_ref)

    def work(role, r):
        def load(b, q):
            at = pl.ds(r * devices + b * half, half)
            return recv[at, q * tiles : (q + 1) * tiles, :].reshape(rows, LANES)

        def store(n, output, begin, value):
            count = value.shape[0] // tiles
            at = pl.ds(r * devices + n * half + begin // tiles, count)
            back[at, output] = value.reshape(count, tiles, LANES)

        correlate(role, load, store, rows, table_refs, scratch)

    def near(mine, r):
        for target in ((0, 1) if mine < 2 else (2, 3)):
            return_to(mine, r, target, 0)
        keep(mine, r).start()

    def far(mine, r, slot):
        for target in ((2, 3) if mine < 2 else (0, 1)):
            return_to(mine, r, target, slot)

    def next_round(r):
        @pl.when(r + AHEAD < plan.rounds)
        def _():
            send_round(r + AHEAD)

    def only(mine, r, body):
        count = plan.counts[mine]
        pl.when((quarter == mine) & (r < count) if count < plan.rounds else quarter == mine)(body)

    @pl.loop(0, plan.rounds)
    def _(r):
        @pl.when(is_lower)
        def _():
            def lower(mine):
                def body():
                    arrived(r, 0, half - 1, height)

                only(mine, r, body)

            lower(0)
            lower(1)
            full = (quarter == 1) & (r < plan.whole)
            if plan.whole:

                @pl.when(full)
                def _():
                    arrived(r, 1, half, height)
                    work("full", r)

            @pl.when(jnp.logical_not(full) & (r < jnp.where(quarter == 0, plan.counts[0], plan.counts[1])))
            def _():
                work("lower", r)

            only(0, r, lambda: near(0, r))
            only(1, r, lambda: near(1, r))
            if plan.whole:
                late = min(FAR_AFTER, plan.rounds - plan.whole)

                @pl.when((quarter == 1) & (r >= late) & (r < late + plan.whole))
                def _():
                    far(1, r - late, 0)

        @pl.when(jnp.logical_not(is_lower))
        def _():
            @pl.when(r < jnp.where(quarter == 2, plan.counts[2], plan.counts[3]))
            def _():
                arrived(r, 0, half, 2 * tiles)
                arrived(r, 1, half - 1, height)
                work("upper", r)

            def upper(mine):
                def body():
                    far(mine, r, 1)
                    near(mine, r)

                only(mine, r, body)

            upper(2)
            upper(3)

        next_round(r)

    def finish(ref, sem):
        pltpu.make_async_copy(ref, ref, sem).wait()

    for mine in range(4):

        @pl.when(quarter == mine)
        def _():
            count = plan.counts[mine]
            finish(land.at[0, :, pl.ds(0, count * tiles), :], own_sem)
            finish(land.at[0, :, pl.ds(0, (channels - count) * tiles), :], land_sem.at[0])
            shared = channels - group * plan.whole
            if mine < 2:
                finish(land.at[1, :, pl.ds(0, shared * tiles), :], land_sem.at[1])
            returned = count * (half - 1)
            if mine == 1:
                returned += plan.whole * half
            elif mine > 1:
                returned += count * half
            finish(back.at[pl.ds(0, returned)], back_sem)
            for target in range(4):
                size = 2 * tiles if mine < 2 and target >= 2 else height
                sent = plan.counts[target] * (group - (mine == target))
                if mine >= 2 and target < 2:
                    sent = plan.whole * group * target
                if sent:
                    finish(recv.at[pl.ds(0, sent), pl.ds(0, size), :], send_sem.at[target])


def spread_kernel(columns, plan, land_ref, out0_ref, out1_ref, result_ref, out_sem):
    _, rows_local, channels = result_ref.shape
    tiles = rows_local // LANES
    me = lax.axis_index("gx") * columns + lax.axis_index("gy")
    is_lower = me < plan.half

    half = rows_local // 2
    shared = lax.broadcasted_iota(jnp.int32, (channels, LANES), 0) % plan.each >= plan.whole

    def run(slots):
        writes = []
        for q, ref in enumerate((out0_ref, out1_ref)):
            for j in range(tiles):
                block = land_ref[0, q, pl.ds(j, channels, stride=tiles), :]
                if slots == 2:
                    more = land_ref[1, q, pl.ds(j, channels, stride=tiles), :]
                    block = block + jnp.where(shared, more, 0.0)
                result_ref[q, j * LANES : (j + 1) * LANES, :] = block.T
                if (j + 1) % (tiles // 2) == 0:
                    at = slice((j + 1) * LANES - half, (j + 1) * LANES)
                    writes.append(
                        pltpu.make_async_copy(
                            result_ref.at[q, at, :], ref.at[at, :], out_sem.at[len(writes)]
                        )
                    )
                    writes[-1].start()
        for copy in writes:
            copy.wait()

    @pl.when(is_lower)
    def _():
        run(2)

    @pl.when(jnp.logical_not(is_lower))
    def _():
        run(1)


def shards(signal, filter_taps, grad_out):
    rows_local, channels = signal.shape
    columns = lax.axis_size("gy")
    devices = lax.axis_size("gx") * columns
    tiles = rows_local // LANES
    plan = Plan(devices, channels)
    rows = plan.half * tiles
    outer, final, inner, turn = make_tables(rows)
    anywhere = pl.BlockSpec(memory_space=pl.ANY)
    result = jax.ShapeDtypeStruct((rows_local, channels), f32)
    land = pl.pallas_call(
        functools.partial(kernel, columns, plan),
        out_shape=pltpu.VMEM((2, 2, channels * tiles, LANES), f32),
        in_specs=[anywhere] * 7,
        out_specs=pl.BlockSpec(memory_space=pltpu.VMEM),
        scratch_shapes=[
            pltpu.VMEM((3, rows_local, channels), f32),
            pltpu.VMEM((channels * 3 * tiles, LANES), f32),
            pltpu.VMEM((plan.rounds * devices, 3 * tiles, LANES), f32),
            pltpu.VMEM((plan.rounds * devices, 2, tiles, LANES), f32),
            pltpu.VMEM(outer.shape, bf16),
            pltpu.VMEM(final.shape, bf16),
            pltpu.VMEM(inner.shape, bf16),
            pltpu.VMEM(turn.shape, f32),
            pltpu.VMEM((2 * rows, 2 * LANES), bf16),
            pltpu.VMEM((2 * rows, 2 * LANES), bf16),
            pltpu.VMEM((rows, 2 * LANES), bf16),
            pltpu.VMEM((rows, 2 * LANES), bf16),
            pltpu.VMEM((4 * rows, 2 * LANES), bf16),
            pltpu.VMEM((4 * rows, 2 * LANES), bf16),
            pltpu.SemaphoreType.DMA((3,)),
            pltpu.SemaphoreType.DMA((4,)),
            pltpu.SemaphoreType.DMA((4,)),
            pltpu.SemaphoreType.DMA((plan.rounds, 2)),
            pltpu.SemaphoreType.DMA,
            pltpu.SemaphoreType.DMA((2,)),
            pltpu.SemaphoreType.DMA,
        ],
        compiler_params=pltpu.CompilerParams(
            collective_id=0, has_side_effects=True, vmem_limit_bytes=58 << 20
        ),
    )(signal, filter_taps, grad_out, outer, final, inner, turn)
    return pl.pallas_call(
        functools.partial(spread_kernel, columns, plan),
        out_shape=(result, result),
        in_specs=[pl.BlockSpec(memory_space=pltpu.VMEM)],
        out_specs=(anywhere, anywhere),
        scratch_shapes=[
            pltpu.VMEM((2, rows_local, channels), f32),
            pltpu.SemaphoreType.DMA((4,)),
        ],
        compiler_params=pltpu.CompilerParams(vmem_limit_bytes=40 << 20),
    )(land)


def solution(mesh):
    spec = P(("gx", "gy"), None)
    return jax.shard_map(
        shards, mesh=mesh, in_specs=(spec,) * 3, out_specs=(spec,) * 2, check_vma=False
    )
```

```python
import functools
import math

import jax
import jax.numpy as jnp
import numpy as np
from jax import lax
from jax.experimental import pallas as pl
from jax.experimental.pallas import tpu as pltpu
from jax.sharding import PartitionSpec as P

LANES = 128
f32, bf16 = jnp.float32, jnp.bfloat16
AHEAD = 4
FAR_AFTER = 4


def halves(table):
    high = table.astype(np.float32).astype(bf16)
    low = (table - high.astype(np.float64)).astype(np.float32).astype(bf16)
    return np.stack([high, low])


def make_tables(rows):
    first = 2 * rows
    period = first * LANES
    angle = 2.0 * math.pi / first * (np.arange(first)[:, None] * np.arange(rows)[None, :] % first)
    c, s = np.cos(angle), np.sin(angle)
    outer = np.block([[c, -s], [s, c]])
    final = np.block([[c.T, -s.T], [s.T, c.T]]) / period
    lane = np.arange(LANES)
    angle = 2.0 * math.pi / LANES * (lane[:, None] * lane[None, :] % LANES)
    c, s = np.cos(angle), np.sin(angle)
    inner = np.block([[c, s], [-s, c]])
    angle = 2.0 * math.pi / period * (np.arange(first)[:, None] * lane[None, :] % period)
    turn = np.stack([np.cos(angle), np.sin(angle)]).astype(np.float32)
    return halves(outer), halves(final), halves(inner), turn


def split(value):
    high = value.astype(bf16)
    return high, (value - high.astype(f32)).astype(bf16)


def mm(a, b):
    return jnp.dot(a, b, preferred_element_type=f32)


class Plan:
    def __init__(self, devices, channels):
        self.devices, self.channels = devices, channels
        self.group = devices // 4
        self.half = 2 * self.group
        self.each = channels // self.group
        self.whole = 3 * self.each // 16
        big = self.each // 2
        small = self.each - self.whole - big
        upper = (big + small + 1) // 2
        self.counts = (big, self.whole + small, upper, big + small - upper)
        self.rounds = max(self.counts)
        self.offsets = (self.whole, big, self.whole, self.whole + upper)

    def channel(self, quarter, place, r):
        offset = self.offsets[quarter] + r
        if quarter == 1 and self.whole:
            offset = jnp.where(r < self.whole, r, offset)
        return place * self.each + offset


def correlate(role, load, store, rows, tables, scratch):
    outer_ref, final_ref, inner_ref, turn_ref = tables
    zh_ref, zl_ref, gh_ref, gl_ref, yh_ref, yl_ref = scratch
    first = 2 * rows
    z_parts = (0,) if role == "lower" else (0, 1)
    g_parts = {"lower": (0,), "upper": (1,), "full": (0, 1)}[role]
    z_width, g_width = len(z_parts) * LANES, len(g_parts) * LANES
    y_width = z_width
    for n, b in enumerate(z_parts):
        at = slice(n * LANES, (n + 1) * LANES)
        for q in range(2):
            down = slice(q * rows, (q + 1) * rows)
            zh_ref[down, at], zl_ref[down, at] = split(load(b, q))
    for n, b in enumerate(g_parts):
        at = slice(n * LANES, (n + 1) * LANES)
        gh_ref[:, at], gl_ref[:, at] = split(load(b, 2))

    def left(table_ref, at, depth, high_ref, low_ref, width):
        high, low = high_ref[:, :width], low_ref[:, :width]
        return (
            mm(table_ref[0, at, :depth], high)
            + mm(table_ref[0, at, :depth], low)
            + mm(table_ref[1, at, :depth], high)
        )

    def right(value):
        high, low = split(value)
        return mm(high, inner_ref[0]) + mm(low, inner_ref[0]) + mm(high, inner_ref[1])

    block = min(first, 256)

    def step(begin):
        real_rows, imag_rows = pl.ds(begin, block), pl.ds(first + begin, block)
        cosine, sine = turn_ref[0, real_rows, :], turn_ref[1, real_rows, :]
        odd = lax.broadcasted_iota(jnp.int32, (block, 2 * LANES), 0) % 2 == 1

        def rotate(real, imag):
            return jnp.concatenate(
                [real * cosine - imag * sine, real * sine + imag * cosine], axis=1
            )

        def spectra(parts, depth, high_ref, low_ref):
            width = len(parts) * LANES
            real = left(outer_ref, real_rows, depth, high_ref, low_ref, width)
            imag = left(outer_ref, imag_rows, depth, high_ref, low_ref, width)
            found = {}
            for n, b in enumerate(parts):
                at = slice(n * LANES, (n + 1) * LANES)
                found[b] = right(rotate(real[:, at], imag[:, at]))
            return found

        z = spectra(z_parts, 2 * rows, zh_ref, zl_ref)
        g = spectra(g_parts, rows, gh_ref, gl_ref)

        def times(z, g):
            zr, zi, gr, gi = z[:, :LANES], z[:, LANES:], g[:, :LANES], g[:, LANES:]
            return jnp.concatenate([zr * gr + zi * gi, zi * gr - zr * gi], axis=1)

        if role == "lower":
            products = [times(z[0], g[0])]
        else:
            across = times(z[0], g[1])
            inside = times(z[1], g[1])
            if role == "full":
                inside = inside + times(z[0], g[0])
            products = [inside + jnp.where(odd, -across, across), across]
        for n, y in enumerate(products):
            y = right(y)
            y = rotate(y[:, :LANES], y[:, LANES:])
            high, low = split(y)
            at = slice(n * LANES, (n + 1) * LANES)
            yh_ref[real_rows, at], yl_ref[real_rows, at] = high[:, :LANES], low[:, :LANES]
            yh_ref[imag_rows, at], yl_ref[imag_rows, at] = high[:, LANES:], low[:, LANES:]

    if block == first:
        step(0)
    else:

        @pl.loop(0, first // block)
        def _(i):
            step(pl.multiple_of(i * block, block))

    block = min(rows, 128)
    for begin in range(0, 2 * rows, block):
        y = left(final_ref, slice(begin, begin + block), 2 * first, yh_ref, yl_ref, y_width)
        for n in range(len(z_parts)):
            store(n, begin // rows, begin % rows, y[:, n * LANES : (n + 1) * LANES])


def kernel(
    columns,
    plan,
    signal_hbm,
    filter_hbm,
    grad_hbm,
    outer_hbm,
    final_hbm,
    inner_hbm,
    turn_hbm,
    land,
    block_ref,
    send,
    recv,
    back,
    outer_ref,
    final_ref,
    inner_ref,
    turn_ref,
    zh_ref,
    zl_ref,
    gh_ref,
    gl_ref,
    yh_ref,
    yl_ref,
    block_sem,
    table_sem,
    send_sem,
    recv_sem,
    back_sem,
    land_sem,
    own_sem,
):
    devices, group, half = plan.devices, plan.group, plan.half
    height = recv.shape[1]
    tiles = height // 3
    rows = half * tiles
    channels = plan.channels
    gx, gy = lax.axis_index("gx"), lax.axis_index("gy")
    me = gx * columns + gy
    deep = group // columns
    quarter, level = gx // deep, gx % deep
    place = level * columns + gy
    is_lower = quarter < 2
    across = [(gy + b) % columns for b in range(columns)]

    def device(peer):
        return (peer // columns, peer % columns)

    def places(body):
        @pl.loop(0, deep)
        def _(a):
            other_level = lax.rem(level + a, deep)
            for b in range(columns):
                body(a == 0 if b == 0 else None, other_level, across[b], other_level * columns + across[b])

    blocks = [
        pltpu.make_async_copy(ref, block_ref.at[q], block_sem.at[q])
        for q, ref in enumerate((filter_hbm, signal_hbm, grad_hbm))
    ]
    for copy in blocks:
        copy.start()
    barrier = pltpu.get_barrier_semaphore()

    def greet(target):
        def body(same, other_level, other_gy, other):
            def signal():
                pl.semaphore_signal(
                    barrier,
                    inc=1,
                    device_id=(target * deep + other_level, other_gy),
                    device_id_type=pl.DeviceIdType.MESH,
                )

            if same is None:
                signal()
            else:
                pl.when(jnp.logical_not(same & (quarter == target)))(signal)

        places(body)

    for target in range(4):
        greet(target)

    tables = [
        pltpu.make_async_copy(a, b, table_sem.at[n])
        for n, (a, b) in enumerate(
            (
                (outer_hbm, outer_ref),
                (final_hbm, final_ref),
                (inner_hbm, inner_ref),
                (turn_hbm, turn_ref),
            )
        )
    ]
    for copy in tables:
        copy.start()
    for q in range(3):
        blocks[q].wait()
        for j in range(tiles):
            block = block_ref[q, j * LANES : (j + 1) * LANES, :].T
            send[pl.ds(q * tiles + j, channels, stride=height), :] = block

    def send_to(target, r, size):
        row = plan.channel(target, 0, r) * height
        arrival = recv.at[r * devices + me, pl.ds(0, size), :]
        sem = recv_sem.at[r, jnp.where(is_lower, 0, 1)]

        def body(same, other_level, other_gy, other):
            def start():
                at = pl.multiple_of(other * (plan.each * height) + row, tiles)
                pltpu.make_async_remote_copy(
                    src_ref=send.at[pl.ds(at, size), :],
                    dst_ref=arrival,
                    send_sem=send_sem.at[target],
                    recv_sem=sem,
                    device_id=(target * deep + other_level, other_gy),
                    device_id_type=pl.DeviceIdType.MESH,
                ).start()

            if same is None:
                start()
            else:
                pl.when(jnp.logical_not(same & (quarter == target)))(start)

        return body

    def send_round(r):
        def guarded(bounds, targets, sizes):
            for target, bound, size in zip(targets, bounds, sizes):
                if bound:

                    @pl.when(r < bound)
                    def _():
                        places(send_to(target, r, size))

        @pl.when(is_lower)
        def _():
            counts = plan.counts
            guarded(
                (counts[0], counts[1], counts[2], counts[3]),
                (0, 1, 2, 3),
                (height, height, 2 * tiles, 2 * tiles),
            )

        @pl.when(jnp.logical_not(is_lower))
        def _():
            guarded((plan.whole, *plan.counts[2:]), (1, 2, 3), (height,) * 3)

    pl.semaphore_wait(barrier, devices - 1)

    @pl.loop(0, min(AHEAD, plan.rounds))
    def _(r):
        send_round(r)

    for mine in range(4):

        @pl.when(quarter == mine)
        def _():
            @pl.loop(0, plan.counts[mine])
            def _(r):
                at = pl.multiple_of(plan.channel(mine, place, r) * height, tiles)
                recv[r * devices + me] = send[pl.ds(at, height), :]

    for copy in tables:
        copy.wait()

    def return_to(mine, r, target, slot):
        at = pl.multiple_of(plan.channel(mine, place, r) * tiles, tiles)
        landing = land.at[slot, :, pl.ds(at, tiles), :]
        base = r * devices + target * group

        def body(same, other_level, other_gy, other):
            def start():
                pltpu.make_async_remote_copy(
                    src_ref=back.at[base + other],
                    dst_ref=landing,
                    send_sem=back_sem,
                    recv_sem=land_sem.at[slot],
                    device_id=(target * deep + other_level, other_gy),
                    device_id_type=pl.DeviceIdType.MESH,
                ).start()

            if same is None or mine != target:
                start()
            else:
                pl.when(jnp.logical_not(same))(start)

        places(body)

    def keep(mine, r):
        at = pl.multiple_of(plan.channel(mine, place, r) * tiles, tiles)
        return pltpu.make_async_copy(
            back.at[r * devices + me], land.at[0, :, pl.ds(at, tiles), :], own_sem
        )

    def arrived(r, source_half, count, size):
        ref = recv.at[pl.ds(0, count), pl.ds(0, size), :]
        pltpu.make_async_copy(ref, ref, recv_sem.at[r, source_half]).wait()

    table_refs = (outer_ref, final_ref, inner_ref, turn_ref)
    scratch = (zh_ref, zl_ref, gh_ref, gl_ref, yh_ref, yl_ref)

    def work(role, r):
        def load(b, q):
            at = pl.ds(r * devices + b * half, half)
            return recv[at, q * tiles : (q + 1) * tiles, :].reshape(rows, LANES)

        def store(n, output, begin, value):
            count = value.shape[0] // tiles
            at = pl.ds(r * devices + n * half + begin // tiles, count)
            back[at, output] = value.reshape(count, tiles, LANES)

        correlate(role, load, store, rows, table_refs, scratch)

    def near(mine, r):
        for target in ((0, 1) if mine < 2 else (2, 3)):
            return_to(mine, r, target, 0)
        keep(mine, r).start()

    def far(mine, r, slot):
        for target in ((2, 3) if mine < 2 else (0, 1)):
            return_to(mine, r, target, slot)

    def next_round(r):
        @pl.when(r + AHEAD < plan.rounds)
        def _():
            send_round(r + AHEAD)

    def only(mine, r, body):
        count = plan.counts[mine]
        pl.when((quarter == mine) & (r < count) if count < plan.rounds else quarter == mine)(body)

    @pl.loop(0, plan.rounds)
    def _(r):
        @pl.when(is_lower)
        def _():
            def lower(mine):
                def body():
                    arrived(r, 0, half - 1, height)

                only(mine, r, body)

            lower(0)
            lower(1)
            next_round(r)
            full = (quarter == 1) & (r < plan.whole)
            if plan.whole:

                @pl.when(full)
                def _():
                    arrived(r, 1, half, height)
                    work("full", r)

            @pl.when(jnp.logical_not(full) & (r < jnp.where(quarter == 0, plan.counts[0], plan.counts[1])))
            def _():
                work("lower", r)

            only(0, r, lambda: near(0, r))
            only(1, r, lambda: near(1, r))
            if plan.whole:
                late = min(FAR_AFTER, plan.rounds - plan.whole)

                @pl.when((quarter == 1) & (r >= late) & (r < late + plan.whole))
                def _():
                    far(1, r - late, 0)

        @pl.when(jnp.logical_not(is_lower))
        def _():
            @pl.when(r < jnp.where(quarter == 2, plan.counts[2], plan.counts[3]))
            def _():
                arrived(r, 0, half, 2 * tiles)
                arrived(r, 1, half - 1, height)

            next_round(r)

            @pl.when(r < jnp.where(quarter == 2, plan.counts[2], plan.counts[3]))
            def _():
                work("upper", r)

            def upper(mine):
                def body():
                    far(mine, r, 1)
                    near(mine, r)

                only(mine, r, body)

            upper(2)
            upper(3)

    def finish(ref, sem):
        pltpu.make_async_copy(ref, ref, sem).wait()

    for mine in range(4):

        @pl.when(quarter == mine)
        def _():
            count = plan.counts[mine]
            finish(land.at[0, :, pl.ds(0, count * tiles), :], own_sem)
            finish(land.at[0, :, pl.ds(0, (channels - count) * tiles), :], land_sem.at[0])
            shared = channels - group * plan.whole
            if mine < 2:
                finish(land.at[1, :, pl.ds(0, shared * tiles), :], land_sem.at[1])
            returned = count * (half - 1)
            if mine == 1:
                returned += plan.whole * half
            elif mine > 1:
                returned += count * half
            finish(back.at[pl.ds(0, returned)], back_sem)
            for target in range(4):
                size = 2 * tiles if mine < 2 and target >= 2 else height
                sent = plan.counts[target] * (group - (mine == target))
                if mine >= 2 and target < 2:
                    sent = plan.whole * group * target
                if sent:
                    finish(recv.at[pl.ds(0, sent), pl.ds(0, size), :], send_sem.at[target])


def spread_kernel(columns, plan, land_ref, out0_ref, out1_ref, result_ref, out_sem):
    _, rows_local, channels = result_ref.shape
    tiles = rows_local // LANES
    me = lax.axis_index("gx") * columns + lax.axis_index("gy")
    is_lower = me < plan.half

    half = rows_local // 2
    shared = lax.broadcasted_iota(jnp.int32, (channels, LANES), 0) % plan.each >= plan.whole

    def run(slots):
        writes = []
        for q, ref in enumerate((out0_ref, out1_ref)):
            for j in range(tiles):
                block = land_ref[0, q, pl.ds(j, channels, stride=tiles), :]
                if slots == 2:
                    more = land_ref[1, q, pl.ds(j, channels, stride=tiles), :]
                    block = block + jnp.where(shared, more, 0.0)
                result_ref[q, j * LANES : (j + 1) * LANES, :] = block.T
                if (j + 1) % (tiles // 2) == 0:
                    at = slice((j + 1) * LANES - half, (j + 1) * LANES)
                    writes.append(
                        pltpu.make_async_copy(
                            result_ref.at[q, at, :], ref.at[at, :], out_sem.at[len(writes)]
                        )
                    )
                    writes[-1].start()
        for copy in writes:
            copy.wait()

    @pl.when(is_lower)
    def _():
        run(2)

    @pl.when(jnp.logical_not(is_lower))
    def _():
        run(1)


def shards(signal, filter_taps, grad_out):
    rows_local, channels = signal.shape
    columns = lax.axis_size("gy")
    devices = lax.axis_size("gx") * columns
    tiles = rows_local // LANES
    plan = Plan(devices, channels)
    rows = plan.half * tiles
    outer, final, inner, turn = make_tables(rows)
    anywhere = pl.BlockSpec(memory_space=pl.ANY)
    result = jax.ShapeDtypeStruct((rows_local, channels), f32)
    land = pl.pallas_call(
        functools.partial(kernel, columns, plan),
        out_shape=pltpu.VMEM((2, 2, channels * tiles, LANES), f32),
        in_specs=[anywhere] * 7,
        out_specs=pl.BlockSpec(memory_space=pltpu.VMEM),
        scratch_shapes=[
            pltpu.VMEM((3, rows_local, channels), f32),
            pltpu.VMEM((channels * 3 * tiles, LANES), f32),
            pltpu.VMEM((plan.rounds * devices, 3 * tiles, LANES), f32),
            pltpu.VMEM((plan.rounds * devices, 2, tiles, LANES), f32),
            pltpu.VMEM(outer.shape, bf16),
            pltpu.VMEM(final.shape, bf16),
            pltpu.VMEM(inner.shape, bf16),
            pltpu.VMEM(turn.shape, f32),
            pltpu.VMEM((2 * rows, 2 * LANES), bf16),
            pltpu.VMEM((2 * rows, 2 * LANES), bf16),
            pltpu.VMEM((rows, 2 * LANES), bf16),
            pltpu.VMEM((rows, 2 * LANES), bf16),
            pltpu.VMEM((4 * rows, 2 * LANES), bf16),
            pltpu.VMEM((4 * rows, 2 * LANES), bf16),
            pltpu.SemaphoreType.DMA((3,)),
            pltpu.SemaphoreType.DMA((4,)),
            pltpu.SemaphoreType.DMA((4,)),
            pltpu.SemaphoreType.DMA((plan.rounds, 2)),
            pltpu.SemaphoreType.DMA,
            pltpu.SemaphoreType.DMA((2,)),
            pltpu.SemaphoreType.DMA,
        ],
        compiler_params=pltpu.CompilerParams(
            collective_id=0, has_side_effects=True, vmem_limit_bytes=58 << 20
        ),
    )(signal, filter_taps, grad_out, outer, final, inner, turn)
    return pl.pallas_call(
        functools.partial(spread_kernel, columns, plan),
        out_shape=(result, result),
        in_specs=[pl.BlockSpec(memory_space=pltpu.VMEM)],
        out_specs=(anywhere, anywhere),
        scratch_shapes=[
            pltpu.VMEM((2, rows_local, channels), f32),
            pltpu.SemaphoreType.DMA((4,)),
        ],
        compiler_params=pltpu.CompilerParams(vmem_limit_bytes=40 << 20),
    )(land)


def solution(mesh):
    spec = P(("gx", "gy"), None)
    return jax.shard_map(
        shards, mesh=mesh, in_specs=(spec,) * 3, out_specs=(spec,) * 2, check_vma=False
    )
```

```python
import functools
import math

import jax
import jax.numpy as jnp
import numpy as np
from jax import lax
from jax.experimental import pallas as pl
from jax.experimental.pallas import tpu as pltpu
from jax.sharding import PartitionSpec as P

LANES = 128
f32, bf16 = jnp.float32, jnp.bfloat16
AHEAD = 4
UPPER_AHEAD = 3
FAR_AFTER = 4


def halves(table):
    high = table.astype(np.float32).astype(bf16)
    low = (table - high.astype(np.float64)).astype(np.float32).astype(bf16)
    return np.stack([high, low])


def make_tables(rows):
    first = 2 * rows
    period = first * LANES
    angle = 2.0 * math.pi / first * (np.arange(first)[:, None] * np.arange(rows)[None, :] % first)
    c, s = np.cos(angle), np.sin(angle)
    outer = np.block([[c, -s], [s, c]])
    final = np.block([[c.T, -s.T], [s.T, c.T]]) / period
    lane = np.arange(LANES)
    angle = 2.0 * math.pi / LANES * (lane[:, None] * lane[None, :] % LANES)
    c, s = np.cos(angle), np.sin(angle)
    inner = np.block([[c, s], [-s, c]])
    angle = 2.0 * math.pi / period * (np.arange(first)[:, None] * lane[None, :] % period)
    turn = np.stack([np.cos(angle), np.sin(angle)]).astype(np.float32)
    return halves(outer), halves(final), halves(inner), turn


def split(value):
    high = value.astype(bf16)
    return high, (value - high.astype(f32)).astype(bf16)


def mm(a, b):
    return jnp.dot(a, b, preferred_element_type=f32)


class Plan:
    def __init__(self, devices, channels):
        self.devices, self.channels = devices, channels
        self.group = devices // 4
        self.half = 2 * self.group
        self.each = channels // self.group
        self.whole = 3 * self.each // 16
        big = self.each // 2
        small = self.each - self.whole - big
        upper = (big + small + 1) // 2
        self.counts = (big, self.whole + small, upper, big + small - upper)
        self.rounds = max(self.counts)
        self.offsets = (self.whole, big, self.whole, self.whole + upper)

    def channel(self, quarter, place, r):
        offset = self.offsets[quarter] + r
        if quarter == 1 and self.whole:
            offset = jnp.where(r < self.whole, r, offset)
        return place * self.each + offset


def correlate(role, load, store, rows, tables, scratch):
    outer_ref, final_ref, inner_ref, turn_ref = tables
    zh_ref, zl_ref, gh_ref, gl_ref, yh_ref, yl_ref = scratch
    first = 2 * rows
    z_parts = (0,) if role == "lower" else (0, 1)
    g_parts = {"lower": (0,), "upper": (1,), "full": (0, 1)}[role]
    z_width, g_width = len(z_parts) * LANES, len(g_parts) * LANES
    y_width = z_width
    for n, b in enumerate(z_parts):
        at = slice(n * LANES, (n + 1) * LANES)
        for q in range(2):
            down = slice(q * rows, (q + 1) * rows)
            zh_ref[down, at], zl_ref[down, at] = split(load(b, q))
    for n, b in enumerate(g_parts):
        at = slice(n * LANES, (n + 1) * LANES)
        gh_ref[:, at], gl_ref[:, at] = split(load(b, 2))

    def left(table_ref, at, depth, high_ref, low_ref, width):
        high, low = high_ref[:, :width], low_ref[:, :width]
        return (
            mm(table_ref[0, at, :depth], high)
            + mm(table_ref[0, at, :depth], low)
            + mm(table_ref[1, at, :depth], high)
        )

    def right(value):
        high, low = split(value)
        return mm(high, inner_ref[0]) + mm(low, inner_ref[0]) + mm(high, inner_ref[1])

    block = min(first, 256)

    def step(begin):
        real_rows, imag_rows = pl.ds(begin, block), pl.ds(first + begin, block)
        cosine, sine = turn_ref[0, real_rows, :], turn_ref[1, real_rows, :]
        odd = lax.broadcasted_iota(jnp.int32, (block, 2 * LANES), 0) % 2 == 1

        def rotate(real, imag):
            return jnp.concatenate(
                [real * cosine - imag * sine, real * sine + imag * cosine], axis=1
            )

        def spectra(parts, depth, high_ref, low_ref):
            width = len(parts) * LANES
            real = left(outer_ref, real_rows, depth, high_ref, low_ref, width)
            imag = left(outer_ref, imag_rows, depth, high_ref, low_ref, width)
            found = {}
            for n, b in enumerate(parts):
                at = slice(n * LANES, (n + 1) * LANES)
                found[b] = right(rotate(real[:, at], imag[:, at]))
            return found

        z = spectra(z_parts, 2 * rows, zh_ref, zl_ref)
        g = spectra(g_parts, rows, gh_ref, gl_ref)

        def times(z, g):
            zr, zi, gr, gi = z[:, :LANES], z[:, LANES:], g[:, :LANES], g[:, LANES:]
            return jnp.concatenate([zr * gr + zi * gi, zi * gr - zr * gi], axis=1)

        if role == "lower":
            products = [times(z[0], g[0])]
        else:
            across = times(z[0], g[1])
            inside = times(z[1], g[1])
            if role == "full":
                inside = inside + times(z[0], g[0])
            products = [inside + jnp.where(odd, -across, across), across]
        for n, y in enumerate(products):
            y = right(y)
            y = rotate(y[:, :LANES], y[:, LANES:])
            high, low = split(y)
            at = slice(n * LANES, (n + 1) * LANES)
            yh_ref[real_rows, at], yl_ref[real_rows, at] = high[:, :LANES], low[:, :LANES]
            yh_ref[imag_rows, at], yl_ref[imag_rows, at] = high[:, LANES:], low[:, LANES:]

    if block == first:
        step(0)
    else:

        @pl.loop(0, first // block)
        def _(i):
            step(pl.multiple_of(i * block, block))

    block = min(rows, 128)
    for begin in range(0, 2 * rows, block):
        y = left(final_ref, slice(begin, begin + block), 2 * first, yh_ref, yl_ref, y_width)
        for n in range(len(z_parts)):
            store(n, begin // rows, begin % rows, y[:, n * LANES : (n + 1) * LANES])


def kernel(
    columns,
    plan,
    signal_hbm,
    filter_hbm,
    grad_hbm,
    outer_hbm,
    final_hbm,
    inner_hbm,
    turn_hbm,
    land,
    block_ref,
    send,
    recv,
    back,
    outer_ref,
    final_ref,
    inner_ref,
    turn_ref,
    zh_ref,
    zl_ref,
    gh_ref,
    gl_ref,
    yh_ref,
    yl_ref,
    block_sem,
    table_sem,
    send_sem,
    recv_sem,
    back_sem,
    land_sem,
    own_sem,
):
    devices, group, half = plan.devices, plan.group, plan.half
    height = recv.shape[1]
    tiles = height // 3
    rows = half * tiles
    channels = plan.channels
    gx, gy = lax.axis_index("gx"), lax.axis_index("gy")
    me = gx * columns + gy
    deep = group // columns
    quarter, level = gx // deep, gx % deep
    place = level * columns + gy
    is_lower = quarter < 2
    across = [(gy + b) % columns for b in range(columns)]

    def device(peer):
        return (peer // columns, peer % columns)

    def places(body):
        @pl.loop(0, deep)
        def _(a):
            other_level = lax.rem(level + a, deep)
            for b in range(columns):
                body(a == 0 if b == 0 else None, other_level, across[b], other_level * columns + across[b])

    blocks = [
        pltpu.make_async_copy(ref, block_ref.at[q], block_sem.at[q])
        for q, ref in enumerate((filter_hbm, signal_hbm, grad_hbm))
    ]
    for copy in blocks:
        copy.start()
    barrier = pltpu.get_barrier_semaphore()

    def greet(target):
        def body(same, other_level, other_gy, other):
            def signal():
                pl.semaphore_signal(
                    barrier,
                    inc=1,
                    device_id=(target * deep + other_level, other_gy),
                    device_id_type=pl.DeviceIdType.MESH,
                )

            if same is None:
                signal()
            else:
                pl.when(jnp.logical_not(same & (quarter == target)))(signal)

        places(body)

    for target in range(4):
        greet(target)

    tables = [
        pltpu.make_async_copy(a, b, table_sem.at[n])
        for n, (a, b) in enumerate(
            (
                (outer_hbm, outer_ref),
                (final_hbm, final_ref),
                (inner_hbm, inner_ref),
                (turn_hbm, turn_ref),
            )
        )
    ]
    for copy in tables:
        copy.start()
    for q in range(3):
        blocks[q].wait()
        for j in range(tiles):
            block = block_ref[q, j * LANES : (j + 1) * LANES, :].T
            send[pl.ds(q * tiles + j, channels, stride=height), :] = block

    def send_to(target, r, size):
        row = plan.channel(target, 0, r) * height
        arrival = recv.at[r * devices + me, pl.ds(0, size), :]
        sem = recv_sem.at[r, jnp.where(is_lower, 0, 1)]

        def body(same, other_level, other_gy, other):
            def start():
                at = pl.multiple_of(other * (plan.each * height) + row, tiles)
                pltpu.make_async_remote_copy(
                    src_ref=send.at[pl.ds(at, size), :],
                    dst_ref=arrival,
                    send_sem=send_sem.at[target],
                    recv_sem=sem,
                    device_id=(target * deep + other_level, other_gy),
                    device_id_type=pl.DeviceIdType.MESH,
                ).start()

            if same is None:
                start()
            else:
                pl.when(jnp.logical_not(same & (quarter == target)))(start)

        return body

    def send_round(r):
        def guarded(bounds, targets, sizes):
            for target, bound, size in zip(targets, bounds, sizes):
                if bound:

                    @pl.when(r < bound)
                    def _():
                        places(send_to(target, r, size))

        @pl.when(is_lower)
        def _():
            counts = plan.counts
            guarded(
                (counts[0], counts[1], counts[2], counts[3]),
                (0, 1, 2, 3),
                (height, height, 2 * tiles, 2 * tiles),
            )

        @pl.when(jnp.logical_not(is_lower))
        def _():
            guarded((plan.whole, *plan.counts[2:]), (1, 2, 3), (height,) * 3)

    pl.semaphore_wait(barrier, devices - 1)

    @pl.loop(0, jnp.where(is_lower, min(AHEAD, plan.rounds), min(UPPER_AHEAD, plan.rounds)))
    def _(r):
        send_round(r)

    for mine in range(4):

        @pl.when(quarter == mine)
        def _():
            @pl.loop(0, plan.counts[mine])
            def _(r):
                at = pl.multiple_of(plan.channel(mine, place, r) * height, tiles)
                recv[r * devices + me] = send[pl.ds(at, height), :]

    for copy in tables:
        copy.wait()

    def return_to(mine, r, target, slot):
        at = pl.multiple_of(plan.channel(mine, place, r) * tiles, tiles)
        landing = land.at[slot, :, pl.ds(at, tiles), :]
        base = r * devices + target * group

        def body(same, other_level, other_gy, other):
            def start():
                pltpu.make_async_remote_copy(
                    src_ref=back.at[base + other],
                    dst_ref=landing,
                    send_sem=back_sem,
                    recv_sem=land_sem.at[slot],
                    device_id=(target * deep + other_level, other_gy),
                    device_id_type=pl.DeviceIdType.MESH,
                ).start()

            if same is None or mine != target:
                start()
            else:
                pl.when(jnp.logical_not(same))(start)

        places(body)

    def keep(mine, r):
        at = pl.multiple_of(plan.channel(mine, place, r) * tiles, tiles)
        return pltpu.make_async_copy(
            back.at[r * devices + me], land.at[0, :, pl.ds(at, tiles), :], own_sem
        )

    def arrived(r, source_half, count, size):
        ref = recv.at[pl.ds(0, count), pl.ds(0, size), :]
        pltpu.make_async_copy(ref, ref, recv_sem.at[r, source_half]).wait()

    table_refs = (outer_ref, final_ref, inner_ref, turn_ref)
    scratch = (zh_ref, zl_ref, gh_ref, gl_ref, yh_ref, yl_ref)

    def work(role, r):
        def load(b, q):
            at = pl.ds(r * devices + b * half, half)
            return recv[at, q * tiles : (q + 1) * tiles, :].reshape(rows, LANES)

        def store(n, output, begin, value):
            count = value.shape[0] // tiles
            at = pl.ds(r * devices + n * half + begin // tiles, count)
            back[at, output] = value.reshape(count, tiles, LANES)

        correlate(role, load, store, rows, table_refs, scratch)

    def near(mine, r):
        for target in ((0, 1) if mine < 2 else (2, 3)):
            return_to(mine, r, target, 0)
        keep(mine, r).start()

    def far(mine, r, slot):
        for target in ((2, 3) if mine < 2 else (0, 1)):
            return_to(mine, r, target, slot)

    def next_upper(r):
        @pl.when(r + UPPER_AHEAD < plan.rounds)
        def _():
            send_round(r + UPPER_AHEAD)

    def next_round(r):
        @pl.when(r + AHEAD < plan.rounds)
        def _():
            send_round(r + AHEAD)

    def only(mine, r, body):
        count = plan.counts[mine]
        pl.when((quarter == mine) & (r < count) if count < plan.rounds else quarter == mine)(body)

    @pl.loop(0, plan.rounds)
    def _(r):
        @pl.when(is_lower)
        def _():
            def lower(mine):
                def body():
                    arrived(r, 0, half - 1, height)

                only(mine, r, body)

            lower(0)
            lower(1)
            next_round(r)
            full = (quarter == 1) & (r < plan.whole)
            if plan.whole:

                @pl.when(full)
                def _():
                    arrived(r, 1, half, height)
                    work("full", r)

            @pl.when(jnp.logical_not(full) & (r < jnp.where(quarter == 0, plan.counts[0], plan.counts[1])))
            def _():
                work("lower", r)

            only(0, r, lambda: near(0, r))
            only(1, r, lambda: near(1, r))
            if plan.whole:
                late = min(FAR_AFTER, plan.rounds - plan.whole)

                @pl.when((quarter == 1) & (r >= late) & (r < late + plan.whole))
                def _():
                    far(1, r - late, 0)

        @pl.when(jnp.logical_not(is_lower))
        def _():
            @pl.when(r < jnp.where(quarter == 2, plan.counts[2], plan.counts[3]))
            def _():
                arrived(r, 0, half, 2 * tiles)
                arrived(r, 1, half - 1, height)

            next_upper(r)

            @pl.when(r < jnp.where(quarter == 2, plan.counts[2], plan.counts[3]))
            def _():
                work("upper", r)

            def upper(mine):
                def body():
                    far(mine, r, 1)
                    near(mine, r)

                only(mine, r, body)

            upper(2)
            upper(3)

    def finish(ref, sem):
        pltpu.make_async_copy(ref, ref, sem).wait()

    for mine in range(4):

        @pl.when(quarter == mine)
        def _():
            count = plan.counts[mine]
            finish(land.at[0, :, pl.ds(0, count * tiles), :], own_sem)
            finish(land.at[0, :, pl.ds(0, (channels - count) * tiles), :], land_sem.at[0])
            shared = channels - group * plan.whole
            if mine < 2:
                finish(land.at[1, :, pl.ds(0, shared * tiles), :], land_sem.at[1])
            returned = count * (half - 1)
            if mine == 1:
                returned += plan.whole * half
            elif mine > 1:
                returned += count * half
            finish(back.at[pl.ds(0, returned)], back_sem)
            for target in range(4):
                size = 2 * tiles if mine < 2 and target >= 2 else height
                sent = plan.counts[target] * (group - (mine == target))
                if mine >= 2 and target < 2:
                    sent = plan.whole * group * target
                if sent:
                    finish(recv.at[pl.ds(0, sent), pl.ds(0, size), :], send_sem.at[target])


def spread_kernel(columns, plan, land_ref, out0_ref, out1_ref, result_ref, out_sem):
    _, rows_local, channels = result_ref.shape
    tiles = rows_local // LANES
    me = lax.axis_index("gx") * columns + lax.axis_index("gy")
    is_lower = me < plan.half

    half = rows_local // 2
    shared = lax.broadcasted_iota(jnp.int32, (channels, LANES), 0) % plan.each >= plan.whole

    def run(slots):
        writes = []
        for q, ref in enumerate((out0_ref, out1_ref)):
            for j in range(tiles):
                block = land_ref[0, q, pl.ds(j, channels, stride=tiles), :]
                if slots == 2:
                    more = land_ref[1, q, pl.ds(j, channels, stride=tiles), :]
                    block = block + jnp.where(shared, more, 0.0)
                result_ref[q, j * LANES : (j + 1) * LANES, :] = block.T
                if (j + 1) % (tiles // 2) == 0:
                    at = slice((j + 1) * LANES - half, (j + 1) * LANES)
                    writes.append(
                        pltpu.make_async_copy(
                            result_ref.at[q, at, :], ref.at[at, :], out_sem.at[len(writes)]
                        )
                    )
                    writes[-1].start()
        for copy in writes:
            copy.wait()

    @pl.when(is_lower)
    def _():
        run(2)

    @pl.when(jnp.logical_not(is_lower))
    def _():
        run(1)


def shards(signal, filter_taps, grad_out):
    rows_local, channels = signal.shape
    columns = lax.axis_size("gy")
    devices = lax.axis_size("gx") * columns
    tiles = rows_local // LANES
    plan = Plan(devices, channels)
    rows = plan.half * tiles
    outer, final, inner, turn = make_tables(rows)
    anywhere = pl.BlockSpec(memory_space=pl.ANY)
    result = jax.ShapeDtypeStruct((rows_local, channels), f32)
    land = pl.pallas_call(
        functools.partial(kernel, columns, plan),
        out_shape=pltpu.VMEM((2, 2, channels * tiles, LANES), f32),
        in_specs=[anywhere] * 7,
        out_specs=pl.BlockSpec(memory_space=pltpu.VMEM),
        scratch_shapes=[
            pltpu.VMEM((3, rows_local, channels), f32),
            pltpu.VMEM((channels * 3 * tiles, LANES), f32),
            pltpu.VMEM((plan.rounds * devices, 3 * tiles, LANES), f32),
            pltpu.VMEM((plan.rounds * devices, 2, tiles, LANES), f32),
            pltpu.VMEM(outer.shape, bf16),
            pltpu.VMEM(final.shape, bf16),
            pltpu.VMEM(inner.shape, bf16),
            pltpu.VMEM(turn.shape, f32),
            pltpu.VMEM((2 * rows, 2 * LANES), bf16),
            pltpu.VMEM((2 * rows, 2 * LANES), bf16),
            pltpu.VMEM((rows, 2 * LANES), bf16),
            pltpu.VMEM((rows, 2 * LANES), bf16),
            pltpu.VMEM((4 * rows, 2 * LANES), bf16),
            pltpu.VMEM((4 * rows, 2 * LANES), bf16),
            pltpu.SemaphoreType.DMA((3,)),
            pltpu.SemaphoreType.DMA((4,)),
            pltpu.SemaphoreType.DMA((4,)),
            pltpu.SemaphoreType.DMA((plan.rounds, 2)),
            pltpu.SemaphoreType.DMA,
            pltpu.SemaphoreType.DMA((2,)),
            pltpu.SemaphoreType.DMA,
        ],
        compiler_params=pltpu.CompilerParams(
            collective_id=0, has_side_effects=True, vmem_limit_bytes=58 << 20
        ),
    )(signal, filter_taps, grad_out, outer, final, inner, turn)
    return pl.pallas_call(
        functools.partial(spread_kernel, columns, plan),
        out_shape=(result, result),
        in_specs=[pl.BlockSpec(memory_space=pltpu.VMEM)],
        out_specs=(anywhere, anywhere),
        scratch_shapes=[
            pltpu.VMEM((2, rows_local, channels), f32),
            pltpu.SemaphoreType.DMA((4,)),
        ],
        compiler_params=pltpu.CompilerParams(vmem_limit_bytes=40 << 20),
    )(land)


def solution(mesh):
    spec = P(("gx", "gy"), None)
    return jax.shard_map(
        shards, mesh=mesh, in_specs=(spec,) * 3, out_specs=(spec,) * 2, check_vma=False
    )
```

```python
import functools
import math

import jax
import jax.numpy as jnp
import numpy as np
from jax import lax
from jax.experimental import pallas as pl
from jax.experimental.pallas import tpu as pltpu
from jax.sharding import PartitionSpec as P

LANES = 128
f32, bf16 = jnp.float32, jnp.bfloat16
AHEAD = 4
UPPER_AHEAD = 3
FAR_AFTER = 5


def halves(table):
    high = table.astype(np.float32).astype(bf16)
    low = (table - high.astype(np.float64)).astype(np.float32).astype(bf16)
    return np.stack([high, low])


def make_tables(rows):
    first = 2 * rows
    period = first * LANES
    angle = 2.0 * math.pi / first * (np.arange(first)[:, None] * np.arange(rows)[None, :] % first)
    c, s = np.cos(angle), np.sin(angle)
    outer = np.block([[c, -s], [s, c]])
    final = np.block([[c.T, -s.T], [s.T, c.T]]) / period
    lane = np.arange(LANES)
    angle = 2.0 * math.pi / LANES * (lane[:, None] * lane[None, :] % LANES)
    c, s = np.cos(angle), np.sin(angle)
    inner = np.block([[c, s], [-s, c]])
    angle = 2.0 * math.pi / period * (np.arange(first)[:, None] * lane[None, :] % period)
    turn = np.stack([np.cos(angle), np.sin(angle)]).astype(np.float32)
    return halves(outer), halves(final), halves(inner), turn


def split(value):
    high = value.astype(bf16)
    return high, (value - high.astype(f32)).astype(bf16)


def mm(a, b):
    return jnp.dot(a, b, preferred_element_type=f32)


class Plan:
    def __init__(self, devices, channels):
        self.devices, self.channels = devices, channels
        self.group = devices // 4
        self.half = 2 * self.group
        self.each = channels // self.group
        self.whole = 3 * self.each // 16
        big = self.each // 2
        small = self.each - self.whole - big
        upper = (big + small + 1) // 2
        self.counts = (big, self.whole + small, upper, big + small - upper)
        self.rounds = max(self.counts)
        self.offsets = (self.whole, big, self.whole, self.whole + upper)

    def channel(self, quarter, place, r):
        offset = self.offsets[quarter] + r
        if quarter == 1 and self.whole:
            offset = jnp.where(r < self.whole, r, offset)
        return place * self.each + offset


def correlate(role, load, store, rows, tables, scratch):
    outer_ref, final_ref, inner_ref, turn_ref = tables
    zh_ref, zl_ref, gh_ref, gl_ref, yh_ref, yl_ref = scratch
    first = 2 * rows
    z_parts = (0,) if role == "lower" else (0, 1)
    g_parts = {"lower": (0,), "upper": (1,), "full": (0, 1)}[role]
    z_width, g_width = len(z_parts) * LANES, len(g_parts) * LANES
    y_width = z_width
    for n, b in enumerate(z_parts):
        at = slice(n * LANES, (n + 1) * LANES)
        for q in range(2):
            down = slice(q * rows, (q + 1) * rows)
            zh_ref[down, at], zl_ref[down, at] = split(load(b, q))
    for n, b in enumerate(g_parts):
        at = slice(n * LANES, (n + 1) * LANES)
        gh_ref[:, at], gl_ref[:, at] = split(load(b, 2))

    def left(table_ref, at, depth, high_ref, low_ref, width):
        high, low = high_ref[:, :width], low_ref[:, :width]
        return (
            mm(table_ref[0, at, :depth], high)
            + mm(table_ref[0, at, :depth], low)
            + mm(table_ref[1, at, :depth], high)
        )

    def right(value):
        high, low = split(value)
        return mm(high, inner_ref[0]) + mm(low, inner_ref[0]) + mm(high, inner_ref[1])

    block = min(first, 256)

    def step(begin):
        real_rows, imag_rows = pl.ds(begin, block), pl.ds(first + begin, block)
        cosine, sine = turn_ref[0, real_rows, :], turn_ref[1, real_rows, :]
        odd = lax.broadcasted_iota(jnp.int32, (block, 2 * LANES), 0) % 2 == 1

        def rotate(real, imag):
            return jnp.concatenate(
                [real * cosine - imag * sine, real * sine + imag * cosine], axis=1
            )

        def spectra(parts, depth, high_ref, low_ref):
            width = len(parts) * LANES
            real = left(outer_ref, real_rows, depth, high_ref, low_ref, width)
            imag = left(outer_ref, imag_rows, depth, high_ref, low_ref, width)
            found = {}
            for n, b in enumerate(parts):
                at = slice(n * LANES, (n + 1) * LANES)
                found[b] = right(rotate(real[:, at], imag[:, at]))
            return found

        z = spectra(z_parts, 2 * rows, zh_ref, zl_ref)
        g = spectra(g_parts, rows, gh_ref, gl_ref)

        def times(z, g):
            zr, zi, gr, gi = z[:, :LANES], z[:, LANES:], g[:, :LANES], g[:, LANES:]
            return jnp.concatenate([zr * gr + zi * gi, zi * gr - zr * gi], axis=1)

        if role == "lower":
            products = [times(z[0], g[0])]
        else:
            across = times(z[0], g[1])
            inside = times(z[1], g[1])
            if role == "full":
                inside = inside + times(z[0], g[0])
            products = [inside + jnp.where(odd, -across, across), across]
        for n, y in enumerate(products):
            y = right(y)
            y = rotate(y[:, :LANES], y[:, LANES:])
            high, low = split(y)
            at = slice(n * LANES, (n + 1) * LANES)
            yh_ref[real_rows, at], yl_ref[real_rows, at] = high[:, :LANES], low[:, :LANES]
            yh_ref[imag_rows, at], yl_ref[imag_rows, at] = high[:, LANES:], low[:, LANES:]

    if block == first:
        step(0)
    else:

        @pl.loop(0, first // block)
        def _(i):
            step(pl.multiple_of(i * block, block))

    block = min(rows, 128)
    for begin in range(0, 2 * rows, block):
        y = left(final_ref, slice(begin, begin + block), 2 * first, yh_ref, yl_ref, y_width)
        for n in range(len(z_parts)):
            store(n, begin // rows, begin % rows, y[:, n * LANES : (n + 1) * LANES])


def kernel(
    columns,
    plan,
    signal_hbm,
    filter_hbm,
    grad_hbm,
    outer_hbm,
    final_hbm,
    inner_hbm,
    turn_hbm,
    land,
    block_ref,
    send,
    recv,
    back,
    outer_ref,
    final_ref,
    inner_ref,
    turn_ref,
    zh_ref,
    zl_ref,
    gh_ref,
    gl_ref,
    yh_ref,
    yl_ref,
    block_sem,
    table_sem,
    send_sem,
    recv_sem,
    back_sem,
    land_sem,
    own_sem,
):
    devices, group, half = plan.devices, plan.group, plan.half
    height = recv.shape[1]
    tiles = height // 3
    rows = half * tiles
    channels = plan.channels
    gx, gy = lax.axis_index("gx"), lax.axis_index("gy")
    me = gx * columns + gy
    deep = group // columns
    quarter, level = gx // deep, gx % deep
    place = level * columns + gy
    is_lower = quarter < 2
    across = [(gy + b) % columns for b in range(columns)]

    def device(peer):
        return (peer // columns, peer % columns)

    def places(body):
        @pl.loop(0, deep)
        def _(a):
            other_level = lax.rem(level + a, deep)
            for b in range(columns):
                body(a == 0 if b == 0 else None, other_level, across[b], other_level * columns + across[b])

    blocks = [
        pltpu.make_async_copy(ref, block_ref.at[q], block_sem.at[q])
        for q, ref in enumerate((filter_hbm, signal_hbm, grad_hbm))
    ]
    for copy in blocks:
        copy.start()
    barrier = pltpu.get_barrier_semaphore()

    def greet(target):
        def body(same, other_level, other_gy, other):
            def signal():
                pl.semaphore_signal(
                    barrier,
                    inc=1,
                    device_id=(target * deep + other_level, other_gy),
                    device_id_type=pl.DeviceIdType.MESH,
                )

            if same is None:
                signal()
            else:
                pl.when(jnp.logical_not(same & (quarter == target)))(signal)

        places(body)

    for target in range(4):
        greet(target)

    tables = [
        pltpu.make_async_copy(a, b, table_sem.at[n])
        for n, (a, b) in enumerate(
            (
                (outer_hbm, outer_ref),
                (final_hbm, final_ref),
                (inner_hbm, inner_ref),
                (turn_hbm, turn_ref),
            )
        )
    ]
    for copy in tables:
        copy.start()
    for q in range(3):
        blocks[q].wait()
        for j in range(tiles):
            block = block_ref[q, j * LANES : (j + 1) * LANES, :].T
            send[pl.ds(q * tiles + j, channels, stride=height), :] = block

    def send_to(target, r, size):
        row = plan.channel(target, 0, r) * height
        arrival = recv.at[r * devices + me, pl.ds(0, size), :]
        sem = recv_sem.at[r, jnp.where(is_lower, 0, 1)]

        def body(same, other_level, other_gy, other):
            def start():
                at = pl.multiple_of(other * (plan.each * height) + row, tiles)
                pltpu.make_async_remote_copy(
                    src_ref=send.at[pl.ds(at, size), :],
                    dst_ref=arrival,
                    send_sem=send_sem.at[target],
                    recv_sem=sem,
                    device_id=(target * deep + other_level, other_gy),
                    device_id_type=pl.DeviceIdType.MESH,
                ).start()

            if same is None:
                start()
            else:
                pl.when(jnp.logical_not(same & (quarter == target)))(start)

        return body

    def send_round(r):
        def guarded(bounds, targets, sizes):
            for target, bound, size in zip(targets, bounds, sizes):
                if bound:

                    @pl.when(r < bound)
                    def _():
                        places(send_to(target, r, size))

        @pl.when(is_lower)
        def _():
            counts = plan.counts
            guarded(
                (counts[0], counts[1], counts[2], counts[3]),
                (0, 1, 2, 3),
                (height, height, 2 * tiles, 2 * tiles),
            )

        @pl.when(jnp.logical_not(is_lower))
        def _():
            guarded((plan.whole, *plan.counts[2:]), (1, 2, 3), (height,) * 3)

    pl.semaphore_wait(barrier, devices - 1)

    @pl.loop(0, jnp.where(is_lower, min(AHEAD, plan.rounds), min(UPPER_AHEAD, plan.rounds)))
    def _(r):
        send_round(r)

    for mine in range(4):

        @pl.when(quarter == mine)
        def _():
            @pl.loop(0, plan.counts[mine])
            def _(r):
                at = pl.multiple_of(plan.channel(mine, place, r) * height, tiles)
                recv[r * devices + me] = send[pl.ds(at, height), :]

    for copy in tables:
        copy.wait()

    def return_to(mine, r, target, slot):
        at = pl.multiple_of(plan.channel(mine, place, r) * tiles, tiles)
        landing = land.at[slot, :, pl.ds(at, tiles), :]
        base = r * devices + target * group

        def body(same, other_level, other_gy, other):
            def start():
                pltpu.make_async_remote_copy(
                    src_ref=back.at[base + other],
                    dst_ref=landing,
                    send_sem=back_sem,
                    recv_sem=land_sem.at[slot],
                    device_id=(target * deep + other_level, other_gy),
                    device_id_type=pl.DeviceIdType.MESH,
                ).start()

            if same is None or mine != target:
                start()
            else:
                pl.when(jnp.logical_not(same))(start)

        places(body)

    def keep(mine, r):
        at = pl.multiple_of(plan.channel(mine, place, r) * tiles, tiles)
        return pltpu.make_async_copy(
            back.at[r * devices + me], land.at[0, :, pl.ds(at, tiles), :], own_sem
        )

    def arrived(r, source_half, count, size):
        ref = recv.at[pl.ds(0, count), pl.ds(0, size), :]
        pltpu.make_async_copy(ref, ref, recv_sem.at[r, source_half]).wait()

    table_refs = (outer_ref, final_ref, inner_ref, turn_ref)
    scratch = (zh_ref, zl_ref, gh_ref, gl_ref, yh_ref, yl_ref)

    def work(role, r):
        def load(b, q):
            at = pl.ds(r * devices + b * half, half)
            return recv[at, q * tiles : (q + 1) * tiles, :].reshape(rows, LANES)

        def store(n, output, begin, value):
            count = value.shape[0] // tiles
            at = pl.ds(r * devices + n * half + begin // tiles, count)
            back[at, output] = value.reshape(count, tiles, LANES)

        correlate(role, load, store, rows, table_refs, scratch)

    def near(mine, r):
        for target in ((0, 1) if mine < 2 else (2, 3)):
            return_to(mine, r, target, 0)
        keep(mine, r).start()

    def far(mine, r, slot):
        for target in ((2, 3) if mine < 2 else (0, 1)):
            return_to(mine, r, target, slot)

    def next_upper(r):
        @pl.when(r + UPPER_AHEAD < plan.rounds)
        def _():
            send_round(r + UPPER_AHEAD)

    def next_round(r):
        @pl.when(r + AHEAD < plan.rounds)
        def _():
            send_round(r + AHEAD)

    def only(mine, r, body):
        count = plan.counts[mine]
        pl.when((quarter == mine) & (r < count) if count < plan.rounds else quarter == mine)(body)

    @pl.loop(0, plan.rounds)
    def _(r):
        @pl.when(is_lower)
        def _():
            def lower(mine):
                def body():
                    arrived(r, 0, half - 1, height)

                only(mine, r, body)

            lower(0)
            lower(1)
            next_round(r)
            full = (quarter == 1) & (r < plan.whole)
            if plan.whole:

                @pl.when(full)
                def _():
                    arrived(r, 1, half, height)
                    work("full", r)

            @pl.when(jnp.logical_not(full) & (r < jnp.where(quarter == 0, plan.counts[0], plan.counts[1])))
            def _():
                work("lower", r)

            only(0, r, lambda: near(0, r))
            only(1, r, lambda: near(1, r))
            if plan.whole:
                late = min(FAR_AFTER, plan.rounds - plan.whole)

                @pl.when((quarter == 1) & (r >= late) & (r < late + plan.whole))
                def _():
                    far(1, r - late, 0)

        @pl.when(jnp.logical_not(is_lower))
        def _():
            @pl.when(r < jnp.where(quarter == 2, plan.counts[2], plan.counts[3]))
            def _():
                arrived(r, 0, half, 2 * tiles)
                arrived(r, 1, half - 1, height)

            next_upper(r)

            @pl.when(r < jnp.where(quarter == 2, plan.counts[2], plan.counts[3]))
            def _():
                work("upper", r)

            def upper(mine):
                def body():
                    far(mine, r, 1)
                    near(mine, r)

                only(mine, r, body)

            upper(2)
            upper(3)

    def finish(ref, sem):
        pltpu.make_async_copy(ref, ref, sem).wait()

    for mine in range(4):

        @pl.when(quarter == mine)
        def _():
            count = plan.counts[mine]
            finish(land.at[0, :, pl.ds(0, count * tiles), :], own_sem)
            finish(land.at[0, :, pl.ds(0, (channels - count) * tiles), :], land_sem.at[0])
            shared = channels - group * plan.whole
            if mine < 2:
                finish(land.at[1, :, pl.ds(0, shared * tiles), :], land_sem.at[1])
            returned = count * (half - 1)
            if mine == 1:
                returned += plan.whole * half
            elif mine > 1:
                returned += count * half
            finish(back.at[pl.ds(0, returned)], back_sem)
            for target in range(4):
                size = 2 * tiles if mine < 2 and target >= 2 else height
                sent = plan.counts[target] * (group - (mine == target))
                if mine >= 2 and target < 2:
                    sent = plan.whole * group * target
                if sent:
                    finish(recv.at[pl.ds(0, sent), pl.ds(0, size), :], send_sem.at[target])


def spread_kernel(columns, plan, land_ref, out0_ref, out1_ref, result_ref, out_sem):
    _, rows_local, channels = result_ref.shape
    tiles = rows_local // LANES
    me = lax.axis_index("gx") * columns + lax.axis_index("gy")
    is_lower = me < plan.half

    half = rows_local // 2
    shared = lax.broadcasted_iota(jnp.int32, (channels, LANES), 0) % plan.each >= plan.whole

    def run(slots):
        writes = []
        for q, ref in enumerate((out0_ref, out1_ref)):
            for j in range(tiles):
                block = land_ref[0, q, pl.ds(j, channels, stride=tiles), :]
                if slots == 2:
                    more = land_ref[1, q, pl.ds(j, channels, stride=tiles), :]
                    block = block + jnp.where(shared, more, 0.0)
                result_ref[q, j * LANES : (j + 1) * LANES, :] = block.T
                if (j + 1) % (tiles // 2) == 0:
                    at = slice((j + 1) * LANES - half, (j + 1) * LANES)
                    writes.append(
                        pltpu.make_async_copy(
                            result_ref.at[q, at, :], ref.at[at, :], out_sem.at[len(writes)]
                        )
                    )
                    writes[-1].start()
        for copy in writes:
            copy.wait()

    @pl.when(is_lower)
    def _():
        run(2)

    @pl.when(jnp.logical_not(is_lower))
    def _():
        run(1)


def shards(signal, filter_taps, grad_out):
    rows_local, channels = signal.shape
    columns = lax.axis_size("gy")
    devices = lax.axis_size("gx") * columns
    tiles = rows_local // LANES
    plan = Plan(devices, channels)
    rows = plan.half * tiles
    outer, final, inner, turn = make_tables(rows)
    anywhere = pl.BlockSpec(memory_space=pl.ANY)
    result = jax.ShapeDtypeStruct((rows_local, channels), f32)
    land = pl.pallas_call(
        functools.partial(kernel, columns, plan),
        out_shape=pltpu.VMEM((2, 2, channels * tiles, LANES), f32),
        in_specs=[anywhere] * 7,
        out_specs=pl.BlockSpec(memory_space=pltpu.VMEM),
        scratch_shapes=[
            pltpu.VMEM((3, rows_local, channels), f32),
            pltpu.VMEM((channels * 3 * tiles, LANES), f32),
            pltpu.VMEM((plan.rounds * devices, 3 * tiles, LANES), f32),
            pltpu.VMEM((plan.rounds * devices, 2, tiles, LANES), f32),
            pltpu.VMEM(outer.shape, bf16),
            pltpu.VMEM(final.shape, bf16),
            pltpu.VMEM(inner.shape, bf16),
            pltpu.VMEM(turn.shape, f32),
            pltpu.VMEM((2 * rows, 2 * LANES), bf16),
            pltpu.VMEM((2 * rows, 2 * LANES), bf16),
            pltpu.VMEM((rows, 2 * LANES), bf16),
            pltpu.VMEM((rows, 2 * LANES), bf16),
            pltpu.VMEM((4 * rows, 2 * LANES), bf16),
            pltpu.VMEM((4 * rows, 2 * LANES), bf16),
            pltpu.SemaphoreType.DMA((3,)),
            pltpu.SemaphoreType.DMA((4,)),
            pltpu.SemaphoreType.DMA((4,)),
            pltpu.SemaphoreType.DMA((plan.rounds, 2)),
            pltpu.SemaphoreType.DMA,
            pltpu.SemaphoreType.DMA((2,)),
            pltpu.SemaphoreType.DMA,
        ],
        compiler_params=pltpu.CompilerParams(
            collective_id=0, has_side_effects=True, vmem_limit_bytes=58 << 20
        ),
    )(signal, filter_taps, grad_out, outer, final, inner, turn)
    return pl.pallas_call(
        functools.partial(spread_kernel, columns, plan),
        out_shape=(result, result),
        in_specs=[pl.BlockSpec(memory_space=pltpu.VMEM)],
        out_specs=(anywhere, anywhere),
        scratch_shapes=[
            pltpu.VMEM((2, rows_local, channels), f32),
            pltpu.SemaphoreType.DMA((4,)),
        ],
        compiler_params=pltpu.CompilerParams(vmem_limit_bytes=40 << 20),
    )(land)


def solution(mesh):
    spec = P(("gx", "gy"), None)
    return jax.shard_map(
        shards, mesh=mesh, in_specs=(spec,) * 3, out_specs=(spec,) * 2, check_vma=False
    )
```
